32 devices in a mesh: ctx: 8 (over z, y), fsdp: 4 (over x, core).
Axes of the slice: x: 2, y: 2, z: 4, core: 2. Of those that a mesh axis runs over, the one named last changes fastest.
Arguments:
- tokens: bfloat16 [4, 2048, 1536], P('fsdp', 'ctx'), may hold values from -6 to 6
- segment_ids: int32 [4, 2048], P('fsdp'), may hold values from 0 to 3, never falling along the last dimension, each value on 1 to 1024 neighbouring positions
- routes: int32 [4, 2048, 2], P('fsdp', 'ctx'), may hold values from 0 to 7, all different within a row; in each aligned block of 256 rows (0 to 255, 256 to 511, ..., all dimensions but the last counted through in order) at most 96 rows name the same one
- upstream: bfloat16 [4, 2048, 1536], P('fsdp', 'ctx'), may hold values from -6 to 6
- step: int32 [6], replicated, may hold values from 1 to 6
- qkv_weight: bfloat16 [1536, 2560], P(('ctx', 'fsdp'))
- qkv_first: float32 [1536, 2560], P(('ctx', 'fsdp'))
- qkv_second: float32 [1536, 2560], P(('ctx', 'fsdp')), may hold values from 20.6848 to 82.7392
- proj_weight: bfloat16 [1536, 1536], P(('ctx', 'fsdp')), may hold values from -1.25 to 1.25
- proj_first: float32 [1536, 1536], P(('ctx', 'fsdp')), may hold values from -4.1815467 to 4.1815467
- proj_second: float32 [1536, 1536], P(('ctx', 'fsdp')), may hold values from 0.4054221 to 1.6216884
- router_weight: bfloat16 [1536, 8], P(('ctx', 'fsdp')), may hold values from -0.15625 to 0.15625
- router_first: float32 [1536, 8], P(('ctx', 'fsdp')), may hold values from -59.73638 to 59.73638
- router_second: float32 [1536, 8], P(('ctx', 'fsdp')), may hold values from 82.7392 to 330.9568
- norm_gains: bfloat16 [1536, 2], P(('ctx', 'fsdp')), may hold values from 0.5 to 1.5
- gains_first: float32 [1536, 2], P(('ctx', 'fsdp')), may hold values from -59.73638 to 59.73638
- gains_second: float32 [1536, 2], P(('ctx', 'fsdp')), may hold values from 82.7392 to 330.9568
- gate_up: bfloat16 [8, 1536, 2048], P('fsdp', 'ctx'), may hold values from -0.15625 to 0.15625
- gate_up_first: float32 [8, 1536, 2048], P('fsdp', 'ctx'), may hold values from -23.894552 to 23.894552
- gate_up_second: float32 [8, 1536, 2048], P('fsdp', 'ctx'), may hold values from 13.238272 to 52.953087
- down_weight: bfloat16 [8, 1024, 1536], P('fsdp', 'ctx'), may hold values from -0.375 to 0.375
- down_first: float32 [8, 1024, 1536], P('fsdp', 'ctx'), may hold values from -7.4670477 to 7.4670477
- down_second: float32 [8, 1024, 1536], P('fsdp', 'ctx'), may hold values from 1.2928 to 5.1712
Outputs:
- block_out: bfloat16 [4, 2048, 1536], P('fsdp', 'ctx')
- token_grad: float32 [4, 2048, 1536], P('fsdp', 'ctx')
- qkv_grad: float32 [1536, 2560], P(('ctx', 'fsdp'))
- proj_grad: float32 [1536, 1536], P(('ctx', 'fsdp'))
- router_grad: float32 [1536, 8], P(('ctx', 'fsdp'))
- gains_grad: float32 [1536, 2], P(('ctx', 'fsdp'))
- gate_up_grad: float32 [8, 1536, 2048], P('fsdp', 'ctx')
- down_grad: float32 [8, 1024, 1536], P('fsdp', 'ctx')
- qkv_first_new: float32 [1536, 2560], P(('ctx', 'fsdp'))
- proj_first_new: float32 [1536, 1536], P(('ctx', 'fsdp'))
- router_first_new: float32 [1536, 8], P(('ctx', 'fsdp'))
- gains_first_new: float32 [1536, 2], P(('ctx', 'fsdp'))
- gate_up_first_new: float32 [8, 1536, 2048], P('fsdp', 'ctx')
- down_first_new: float32 [8, 1024, 1536], P('fsdp', 'ctx')
- qkv_second_new: float32 [1536, 2560], P(('ctx', 'fsdp'))
- proj_second_new: float32 [1536, 1536], P(('ctx', 'fsdp'))
- router_second_new: float32 [1536, 8], P(('ctx', 'fsdp'))
- gains_second_new: float32 [1536, 2], P(('ctx', 'fsdp'))
- gate_up_second_new: float32 [8, 1536, 2048], P('fsdp', 'ctx')
- down_second_new: float32 [8, 1024, 1536], P('fsdp', 'ctx')
- qkv_new: float32 [1536, 2560], P(('ctx', 'fsdp'))
- proj_new: float32 [1536, 1536], P(('ctx', 'fsdp'))
- router_new: float32 [1536, 8], P(('ctx', 'fsdp'))
- gains_new: float32 [1536, 2], P(('ctx', 'fsdp'))
- gate_up_new: float32 [8, 1536, 2048], P('fsdp', 'ctx')
- down_new: float32 [8, 1024, 1536], P('fsdp', 'ctx')
- matrix_norms: float32 [2, 6], replicated
The draws below stay inside these ranges and needn't reach their ends.
Inputs may be any that keep to these rules, and one draw needn't show every extreme that they name: `segment_ids`: in each sequence the numbers never fall, and each document holds 1 to 1024 consecutive tokens, one exactly 1024. `routes`: each token names two different experts; within the tokens of one device (aligned blocks of 256 tokens) no expert is named more than 96 times, a bound that some block reaches.
All inputs are finite; a program needn't handle non-finite values.
Results may differ from the reference program's by a relative error of at most 0.019.
Values may be sent and summed in bfloat16 or wider, within the bound.
No kernel may reach another device: no remote copies, remote signals or barrier semaphores. Data moves between devices by JAX's collectives and lax.ppermute only.
A program may use at most 256 MiB of HBM per device.

```python
import math
import jax
import jax.numpy as jnp
import numpy as np
from jax import lax

D = 1536
KEY_HEADS = 8
HEAD_WIDTH = 64
FF = 1024
TOK_DEV = 256
QUERY_PER_KEY = 3
QUERY_CHANNELS = 1536
KEY_CHANNELS = 512
SEQUENCE_TOKENS = 2048
SEQUENCE_COUNT = 4
EXPERTS = 8
CAP = 96
SEG_COUNT = 4
SEG_MOST = 1024
N_CTX = 8


def rising_rows(count, upper_ratio):
    place = jnp.arange(count, dtype=jnp.float32) / max(count - 1, 1)
    mean_square = (upper_ratio - 1.0 / upper_ratio) / (2.0 * math.log(upper_ratio))
    return jnp.power(upper_ratio, place - 0.5) / math.sqrt(mean_square)


def draw_qkv_weight(key, part):
    upper_ratio = 3.0
    values = jnp.clip(jax.random.normal(key, (D, QUERY_CHANNELS + 2 * KEY_CHANNELS), jnp.float32), -5.0, 5.0)
    return (values * rising_rows(D, upper_ratio)[:, None] * D ** (-0.5)).astype(jnp.bfloat16)


def draw_qkv_first(key, part):
    upper_ratio = 3.0
    values = jnp.clip(jax.random.normal(key, (D, QUERY_CHANNELS + 2 * KEY_CHANNELS), jnp.float32), -5.0, 5.0)
    return values * rising_rows(D, upper_ratio)[:, None] * (0.055 * (SEQUENCE_COUNT * SEQUENCE_TOKENS) ** 0.5)


def plant(values, stream_key, least, high):
    dims = values.shape
    spot = [jax.random.randint(jax.random.fold_in(stream_key, axis), (), 0, dims[axis]) for axis in range(len(dims))]
    values = values.at[tuple(spot)].set(least)
    longest = dims.index(max(dims))
    spot[longest] = (spot[longest] + 1) % dims[longest]
    return values.at[tuple(spot)].set(high)


def level_of(stream_key, shape, shards, low, top_value):
    def one(position, blocks):
        draws = jax.random.uniform(jax.random.fold_in(jax.random.fold_in(stream_key, 6), position), (blocks,), jnp.float32, low / len(shards), top_value / len(shards))
        return jnp.repeat(jnp.exp(draws), shape[position] // blocks).reshape((-1,) + (1,) * (len(shape) - position - 1))

    gain = one(*shards[0])
    for cut in shards[1:]:
        gain = gain * one(*cut)
    return gain


def split_up(amount, total, reach, skew):
    weights = [(1 << 20) // math.isqrt(standing ** skew) + 1 for standing in range(2, amount + 1)]
    rest, given = total - reach - (amount - 1), [1] * (amount - 1)
    while rest > 0:
        candidates = [i for i in range(amount - 1) if given[i] < reach]
        whole, left = sum([weights[i] for i in candidates]), rest
        for i in candidates:
            extra = min(reach - given[i], max(1, left * weights[i] // whole), rest)
            given[i] = given[i] + extra
            rest = rest - extra
    return np.array([reach] + given)


def uneven(own_key, number_of, total, reach, lean):
    if number_of == 2:
        one = jax.random.randint(own_key, (), max(1, total - reach), min(reach, total - 1) + 1)
        return jnp.stack([one, total - one])
    sizes = jnp.asarray(split_up(number_of, total, reach, lean), jnp.int32)
    pairs = (number_of - 1) // 2
    giver, sink = sizes[1:1 + 2 * pairs:2], sizes[2:2 + 2 * pairs:2]
    room = jnp.minimum(giver - 1, reach - sink)
    passed = jax.random.randint(jax.random.fold_in(own_key, 1), (pairs,), 0, 1 << 20) % (room + 1)
    sizes = sizes.at[1:1 + 2 * pairs:2].set(giver - passed).at[2:2 + 2 * pairs:2].set(sink + passed)
    return sizes[jax.random.permutation(jax.random.fold_in(own_key, 2), number_of)]


def shared_out(rng, own, number, rows, number_of, top, most, skew):
    sequence = jax.random.permutation(rng, number_of)
    packed, ordinary = load_shares(number_of, rows * top, most, skew, True), load_shares(number_of, rows * top, most, skew, False)
    places = jnp.arange(number_of)

    def named(tallies, rotation):
        used = int((tallies > 0).sum())
        fixed = max(1, used // 4)
        moved = fixed + (places - fixed + rotation * (used - fixed)) % max(1, number_of - fixed)
        return jnp.zeros((number_of,), jnp.int32).at[sequence[jnp.where(places < fixed, places, moved)]].set(jnp.asarray(tallies, jnp.int32))

    tallies = jnp.where(number % 4 == 0, named(packed, number // 4), named(ordinary, number - number // 4 - 1))
    mixed = jax.random.permutation(jax.random.fold_in(own, 3), number_of)
    donor, sink = mixed[0:number_of // 2 * 2:2], mixed[1:number_of // 2 * 2:2]
    margin = jnp.minimum(tallies[donor] - 1, most - tallies[sink]) // 2
    margin = jnp.where((donor == sequence[0]) | (sink == sequence[0]) | (tallies[sink] == 0), 0, jnp.maximum(margin, 0))
    moved = jax.random.randint(jax.random.fold_in(own, 4), (number_of // 2,), 0, 1 << 20) % (margin + 1)
    tallies = tallies.at[donor].add(-moved).at[sink].add(moved)
    members = jnp.searchsorted(jnp.cumsum(tallies), jnp.arange(rows * top), side="right").astype(jnp.int32)
    listing = members.reshape(top, rows).T
    listing = listing[jax.random.permutation(jax.random.fold_in(own, 1), rows)]
    rotation = jax.random.randint(jax.random.fold_in(own, 2), (rows, 1), 0, top)
    return jnp.take_along_axis(listing, (jnp.arange(top)[None, :] + rotation) % top, axis=1)


def load_shares(number_of, total, most, slope, full):
    loads = [(1 << 20) // math.isqrt(standing ** slope) + 1 for standing in range(1, number_of + 1)]
    largest = most if full else min(most, max(-(-total // number_of), total * loads[0] // sum(loads)))
    least = 1 if total - largest >= number_of - 1 else 0
    given, rest = [largest] + [least] * (number_of - 1), total - largest - least * (number_of - 1)
    while rest > 0:
        movable = [i for i in range(1, number_of) if given[i] < largest] or [i for i in range(1, number_of) if given[i] < most]
        pool, remaining = sum([loads[i] for i in movable]), rest
        for i in movable:
            extra = min(most - given[i], max(1, remaining * loads[i] // pool), rest)
            given[i] = given[i] + extra
            rest = rest - extra
    return np.array(given)


def gaussian(stream_key, dims, width, reach, cuts=(), held_as=jnp.bfloat16):
    values = jax.random.normal(stream_key, dims, jnp.float32) * width
    if len(cuts) > 0:
        values = level_of(stream_key, dims, cuts, -0.22, 0.18) * values
    return jnp.clip(values, min=-reach, max=reach).astype(held_as)


def setup_inputs(seed: int = 0) -> dict:
    key_of = jax.random.split(jax.random.key(seed), 24)
    tokens = gaussian(key_of[0], (SEQUENCE_COUNT, SEQUENCE_TOKENS, D), 1.0, 6.0, ((0, 4), (1, 8)))
    segment_ids = jax.vmap(lambda own: jnp.searchsorted(jnp.cumsum(uneven(own, SEG_COUNT, SEQUENCE_TOKENS, SEG_MOST, 1)), jnp.arange(SEQUENCE_TOKENS), side="right"))(jax.random.split(key_of[1], SEQUENCE_COUNT)).reshape((SEQUENCE_COUNT, SEQUENCE_TOKENS)).astype(jnp.int32)
    routes_keys = jax.random.split(jax.random.fold_in(key_of[2], 1), SEQUENCE_COUNT * SEQUENCE_TOKENS // TOK_DEV)
    routes_turns = jax.random.permutation(jax.random.fold_in(key_of[2], 3), SEQUENCE_COUNT * SEQUENCE_TOKENS // TOK_DEV)
    routes = jax.vmap(lambda own, number: shared_out(jax.random.fold_in(key_of[2], 2), own, number, TOK_DEV, EXPERTS, 2, CAP, 1))(routes_keys, routes_turns).reshape((SEQUENCE_COUNT, SEQUENCE_TOKENS, 2))
    upstream = gaussian(key_of[3], (SEQUENCE_COUNT, SEQUENCE_TOKENS, D), 1.0, 6.0, ((0, 4), (1, 8)))
    step = plant(jax.random.randint(key_of[4], (6,), 1, 7), jax.random.fold_in(key_of[4], 1), 1, 6).astype(jnp.int32)
    qkv_weight = draw_qkv_weight(jax.random.fold_in(key_of[23], 71), 0)
    qkv_first = draw_qkv_first(jax.random.fold_in(key_of[23], 71), 0)
    qkv_second = jnp.clip(jnp.exp(math.log(82.7392) - 1.3862944 * jax.random.uniform(key_of[7], (D, QUERY_CHANNELS + 2 * KEY_CHANNELS), jnp.float32) ** level_of(key_of[7], (D, QUERY_CHANNELS + 2 * KEY_CHANNELS), ((0, 32),), -0.2, 0.2)), 20.6848, 82.7392)
    proj_weight = gaussian(key_of[8], (D, QUERY_CHANNELS), (QUERY_CHANNELS // 64) ** -0.5, 1.25, ((0, 32),))
    proj_first = gaussian(key_of[9], (D, QUERY_CHANNELS), (0.11 * 0.07 * (SEQUENCE_COUNT * SEQUENCE_TOKENS) ** 0.5), 4.1815467, ((0, 32),), jnp.float32)
    proj_second = jnp.clip(jnp.exp(math.log(1.6216884) - 1.3862944 * jax.random.uniform(key_of[10], (D, QUERY_CHANNELS), jnp.float32) ** level_of(key_of[10], (D, QUERY_CHANNELS), ((0, 32),), -0.2, 0.2)), 0.4054221, 1.6216884)
    router_weight = gaussian(key_of[11], (D, EXPERTS), D ** -0.5, 0.15625, ((0, 32),))
    router_first = gaussian(key_of[12], (D, EXPERTS), (0.11 * (SEQUENCE_COUNT * SEQUENCE_TOKENS) ** 0.5), 59.73638, ((0, 32),), jnp.float32)
    router_second = jnp.clip(jnp.exp(math.log(330.9568) - 1.3862944 * jax.random.uniform(key_of[13], (D, EXPERTS), jnp.float32) ** level_of(key_of[13], (D, EXPERTS), ((0, 32),), -0.2, 0.2)), 82.7392, 330.9568)
    norm_gains = jnp.clip(1.0 + 0.1 * jax.random.normal(key_of[14], (D, 2), jnp.float32), 0.5, 1.5).astype(jnp.bfloat16)
    gains_first = gaussian(key_of[15], (D, 2), (0.11 * (SEQUENCE_COUNT * SEQUENCE_TOKENS) ** 0.5), 59.73638, ((0, 32),), jnp.float32)
    gains_second = jnp.clip(jnp.exp(math.log(330.9568) - 1.3862944 * jax.random.uniform(key_of[16], (D, 2), jnp.float32) ** level_of(key_of[16], (D, 2), ((0, 32),), -0.2, 0.2)), 82.7392, 330.9568)
    gate_up = gaussian(key_of[17], (EXPERTS, D, 2 * FF), D ** -0.5, 0.15625, ((0, 4), (1, 8)))
    gate_up_first = gaussian(key_of[18], (EXPERTS, D, 2 * FF), (0.11 * 0.8 * (2 * SEQUENCE_COUNT * SEQUENCE_TOKENS / EXPERTS) ** 0.5), 23.894552, ((0, 4), (1, 8)), jnp.float32)
    gate_up_second = jnp.clip(jnp.exp(math.log(52.953087) - 1.3862944 * jax.random.uniform(key_of[19], (EXPERTS, D, 2 * FF), jnp.float32) ** level_of(key_of[19], (EXPERTS, D, 2 * FF), ((0, 4), (1, 8)), -0.2, 0.2)), 13.238272, 52.953087)
    down_weight = gaussian(key_of[20], (EXPERTS, FF, D), (FF // 4) ** -0.5, 0.375, ((0, 4), (1, 8)))
    down_first = gaussian(key_of[21], (EXPERTS, FF, D), (0.11 * 0.25 * (2 * SEQUENCE_COUNT * SEQUENCE_TOKENS / EXPERTS) ** 0.5), 7.4670477, ((0, 4), (1, 8)), jnp.float32)
    down_second = jnp.clip(jnp.exp(math.log(5.1712) - 1.3862944 * jax.random.uniform(key_of[22], (EXPERTS, FF, D), jnp.float32) ** level_of(key_of[22], (EXPERTS, FF, D), ((0, 4), (1, 8)), -0.2, 0.2)), 1.2928, 5.1712)
    return dict(tokens=tokens, segment_ids=segment_ids, routes=routes, upstream=upstream, step=step, qkv_weight=qkv_weight, qkv_first=qkv_first, qkv_second=qkv_second, proj_weight=proj_weight, proj_first=proj_first, proj_second=proj_second, router_weight=router_weight, router_first=router_first, router_second=router_second, norm_gains=norm_gains, gains_first=gains_first, gains_second=gains_second, gate_up=gate_up, gate_up_first=gate_up_first, gate_up_second=gate_up_second, down_weight=down_weight, down_first=down_first, down_second=down_second)


norm_epsilon = 1e-05
beta_first = 0.9
beta_second = 0.99
adam_epsilon = 1e-08
weight_decay = 0.01
learn_rate = 0.5
ratio_epsilon = 1e-06
score_masked = -1e+30
highest_mode = lax.Precision.HIGHEST

@jax.custom_vjp
def low(v):
    return lax.optimization_barrier(v.astype(jnp.bfloat16)).astype(jnp.float32)

@jax.custom_vjp
def low_back(v):
    return v

def low_keep(v):
    return (low(v), None)

def low_pass(kept, grad):
    return (grad,)

def back_keep(v):
    return (v, None)

def back_low(kept, grad):
    return (low(grad),)
low.defvjp(low_keep, low_pass)
low_back.defvjp(back_keep, back_low)

def rms_norm(values, gain_vec):
    scaling = lax.rsqrt(lax.optimization_barrier(jnp.mean(values * values, axis=-1, keepdims=True)) + norm_epsilon)
    return values * scaling * gain_vec

def matmul(left_side, right_side):
    return jnp.dot(left_side, right_side, precision=highest_mode, preferred_element_type=jnp.float32)

def attend_sequence(operands):
    query_rows, keys_seq, values_seq, segments = operands
    block_row_span = min(512, SEQUENCE_TOKENS)
    positions = jnp.arange(SEQUENCE_TOKENS, dtype=jnp.int32)

    def one_block(start_row):
        query_block = lax.dynamic_slice_in_dim(query_rows, start_row, block_row_span, 0)
        query_seg = lax.dynamic_slice_in_dim(segments, start_row, block_row_span, 0)
        query_pos = start_row + jnp.arange(block_row_span, dtype=jnp.int32)
        scores = low_back(jnp.einsum('qhgd,khd->hgqk', query_block, keys_seq, precision=highest_mode) * 0.125)
        allowed = (positions[None, :] <= query_pos[:, None]) & (segments[None, :] == query_seg[:, None])
        attention = jax.nn.softmax(jnp.where(allowed, scores, score_masked), axis=-1)
        return jnp.einsum('hgqk,khd->qhgd', low(attention), values_seq, precision=highest_mode)
    starts = (jnp.arange(SEQUENCE_TOKENS // block_row_span) * block_row_span).astype(jnp.int32)
    return lax.map(jax.checkpoint(one_block), starts).reshape(SEQUENCE_TOKENS, QUERY_CHANNELS)

def slot_positions(routes):
    blocks = SEQUENCE_COUNT * N_CTX
    flat_routes = routes.reshape(blocks, TOK_DEV * 2)
    onehot = (flat_routes[:, :, None] == jnp.arange(EXPERTS, dtype=jnp.int32)[None, None, :]).astype(jnp.int32)
    earlier = jnp.cumsum(onehot, axis=1) - onehot
    slot_rank = lax.optimization_barrier(jnp.sum(earlier * onehot, axis=2))
    owners = jnp.arange(blocks, dtype=jnp.int32)[:, None]
    return ((owners * EXPERTS + flat_routes) * CAP + slot_rank).reshape(-1).astype(jnp.int32)

def expert_apply(operands):
    rows_in, gate_weights, down_part = operands
    both_parts = low_back(matmul(rows_in, gate_weights))
    activated = low(jax.nn.silu(both_parts[:, :FF]) * both_parts[:, FF:])
    return low(low_back(matmul(activated, down_part)))

def forward(params, tokens, segment_ids, routes, positions):
    qkv_weight, proj_weight, router_weight, norm_gains, gate_up, down_weight = params
    blocks = SEQUENCE_COUNT * N_CTX
    flat_tokens = tokens.reshape(SEQUENCE_COUNT * SEQUENCE_TOKENS, D)
    hidden = low(rms_norm(flat_tokens, norm_gains[:, 0]))
    blended_rows = low(low_back(matmul(hidden, qkv_weight)))
    query_rows = blended_rows[:, :QUERY_CHANNELS].reshape(SEQUENCE_COUNT, SEQUENCE_TOKENS, KEY_HEADS, QUERY_PER_KEY, HEAD_WIDTH)
    every_key_row = blended_rows[:, QUERY_CHANNELS:QUERY_CHANNELS + KEY_CHANNELS].reshape(SEQUENCE_COUNT, SEQUENCE_TOKENS, KEY_HEADS, HEAD_WIDTH)
    every_value_row = blended_rows[:, QUERY_CHANNELS + KEY_CHANNELS:].reshape(SEQUENCE_COUNT, SEQUENCE_TOKENS, KEY_HEADS, HEAD_WIDTH)
    attended = lax.map(attend_sequence, (query_rows, every_key_row, every_value_row, segment_ids))
    attended = low(low_back(attended.reshape(SEQUENCE_COUNT * SEQUENCE_TOKENS, QUERY_CHANNELS)))
    branch = low_back(lax.dot_general(attended, proj_weight, (((1,), (1,)), ((), ())), precision=highest_mode, preferred_element_type=jnp.float32))
    middle = flat_tokens + branch
    second = low(rms_norm(middle, norm_gains[:, 1]))
    probabilities = jax.nn.softmax(matmul(second, router_weight), axis=-1)
    chosen = routes.reshape(SEQUENCE_COUNT * SEQUENCE_TOKENS, 2)[:, :, None] == jnp.arange(EXPERTS, dtype=jnp.int32)[None, None, :]
    picked = lax.optimization_barrier(jnp.sum(jnp.where(chosen, probabilities[:, None, :], 0.0), axis=2))
    combine = picked / lax.optimization_barrier(jnp.sum(picked, axis=1, keepdims=True))
    copies = low_back(jnp.repeat(second, 2, axis=0))
    buffer = jnp.zeros((blocks * EXPERTS * CAP, D), second.dtype).at[positions].set(copies)
    buffer = buffer.reshape(blocks, EXPERTS, CAP, D).transpose(1, 0, 2, 3).reshape(EXPERTS, blocks * CAP, D)
    produced = lax.map(jax.checkpoint(expert_apply), (buffer, gate_up, down_weight))
    produced = produced.reshape(EXPERTS, blocks, CAP, D).transpose(1, 0, 2, 3).reshape(blocks * EXPERTS * CAP, D)
    returned = produced[positions].reshape(SEQUENCE_COUNT * SEQUENCE_TOKENS, 2, D)
    result = middle + lax.optimization_barrier(jnp.sum(combine[:, :, None] * returned, axis=1))
    return result.reshape(SEQUENCE_COUNT, SEQUENCE_TOKENS, D)

def adam_ratio(tensor, gradient, first_old, second_old, step_count):
    bias_one = 1.0 - jnp.power(beta_first, step_count)
    bias_two = 1.0 - jnp.power(beta_second, step_count)
    first_new = beta_first * first_old + (1.0 - beta_first) * gradient
    second_new = beta_second * second_old + (1.0 - beta_second) * gradient * gradient
    step_ratio = first_new / bias_one / (jnp.sqrt(second_new / bias_two) + adam_epsilon) + weight_decay * tensor
    return (first_new, second_new, step_ratio)

def reference(tokens, segment_ids, routes, upstream, step, qkv_weight, qkv_first, qkv_second, proj_weight, proj_first, proj_second, router_weight, router_first, router_second, norm_gains, gains_first, gains_second, gate_up, gate_up_first, gate_up_second, down_weight, down_first, down_second):
    weights = (qkv_weight, proj_weight, router_weight, norm_gains, gate_up, down_weight)
    params = tuple((tensor.astype(jnp.float32) for tensor in weights))
    positions = slot_positions(routes)

    def apply_layer(param_list, inputs):
        return forward(param_list, inputs, segment_ids, routes, positions)
    result, pullback = jax.vjp(apply_layer, params, tokens.astype(jnp.float32))
    param_grads, token_grad = pullback(upstream.astype(jnp.float32))
    firsts = (qkv_first, proj_first, router_first, gains_first, gate_up_first, down_first)
    seconds = (qkv_second, proj_second, router_second, gains_second, gate_up_second, down_second)
    step_counts = step.astype(jnp.float32)
    states = [adam_ratio(params[number], param_grads[number], firsts[number], seconds[number], step_counts[number]) for number in range(6)]
    weight_sq = jnp.stack([jnp.sum(tensor * tensor) for tensor in params])
    ratio_sq = jnp.stack([jnp.sum(entry[2] * entry[2]) for entry in states])
    trust_ratio = jnp.sqrt(weight_sq) * lax.rsqrt(ratio_sq + ratio_epsilon)
    new_weights = [params[number] - learn_rate * trust_ratio[number] * states[number][2] for number in range(6)]
    matrix_norms = 0.5 * jnp.log(jnp.stack([weight_sq, ratio_sq + ratio_epsilon]))
    return (result.astype(jnp.bfloat16), token_grad, param_grads[0], param_grads[1], param_grads[2], param_grads[3], param_grads[4], param_grads[5], states[0][0], states[1][0], states[2][0], states[3][0], states[4][0], states[5][0], states[0][1], states[1][1], states[2][1], states[3][1], states[4][1], states[5][1], new_weights[0], new_weights[1], new_weights[2], new_weights[3], new_weights[4], new_weights[5], matrix_norms)
```

```python
import functools

import jax
import jax.numpy as jnp
from jax import lax
from jax.experimental import pallas as pl
from jax.experimental.pallas import tpu as pltpu
from jax.sharding import PartitionSpec as P

KEY_HEADS = 8
HEAD_WIDTH = 64
FF = 1024
QUERY_PER_KEY = 3
QUERY_CHANNELS = 1536
KEY_CHANNELS = 512

norm_epsilon = 1e-05
beta_first = 0.9
beta_second = 0.99
adam_epsilon = 1e-08
weight_decay = 0.01
learn_rate = 0.5
ratio_epsilon = 1e-06
score_masked = -1e30
highest_mode = lax.Precision.HIGHEST


BF = jnp.bfloat16
F32 = jnp.float32
AXES = ("ctx", "fsdp")


def rms_norm(values, gain_vec):
    scaling = lax.rsqrt(jnp.mean(values * values, axis=-1, keepdims=True) + norm_epsilon)
    return values * scaling * gain_vec


def routing(logits, chosen):
    probabilities = jax.nn.softmax(logits, axis=-1)
    picked = jnp.sum(jnp.where(chosen, probabilities[:, None, :], 0.0), axis=2)
    return picked / jnp.sum(picked, axis=1, keepdims=True)


def adam_ratio(weight, gradient, first_old, second_old, step_count):
    tensor = weight.astype(F32)
    bias_one = 1.0 - jnp.power(beta_first, step_count)
    bias_two = 1.0 - jnp.power(beta_second, step_count)
    first_new = beta_first * first_old + (1.0 - beta_first) * gradient
    second_new = beta_second * second_old + (1.0 - beta_second) * gradient * gradient
    step_ratio = (
        first_new / bias_one / (jnp.sqrt(second_new / bias_two) + adam_epsilon)
        + weight_decay * tensor
    )
    return (first_new, second_new, step_ratio)


def nt(left, right):
    return lax.dot_general(left, right, (((1,), (1,)), ((), ())), preferred_element_type=F32)


def tn(left, right):
    return lax.dot_general(left, right, (((0,), (0,)), ((), ())), preferred_element_type=F32)


def nn(left, right):
    return jnp.dot(left, right, preferred_element_type=F32)


def three(ref, head, rows):
    base = head * QUERY_PER_KEY * HEAD_WIDTH
    return jnp.concatenate(
        [
            ref[:, base + g * HEAD_WIDTH : base + (g + 1) * HEAD_WIDTH]
            for g in range(QUERY_PER_KEY)
        ],
        axis=0,
    )


def put_three(ref, head, rows, turned):
    base = head * QUERY_PER_KEY * HEAD_WIDTH
    for g in range(QUERY_PER_KEY):
        part = turned[:, g * rows : (g + 1) * rows]
        ref[:, base + g * HEAD_WIDTH : base + (g + 1) * HEAD_WIDTH] = part.T.astype(ref.dtype)


def fill_bias(low_ref, bias, rows, window):
    @pl.when(pl.program_id(0) == 0)
    def _():
        def step(block, _):
            start = pl.multiple_of(block * rows, rows)
            key_pos = start + lax.broadcasted_iota(jnp.int32, (rows, rows), 0)
            top = lax.broadcasted_iota(jnp.int32, (rows, rows), 1) + (window - rows)
            allowed = (key_pos >= low_ref[...]) & (key_pos <= top)
            bias[pl.ds(start, rows), :] = jnp.where(allowed, 0.0, score_masked)
            return 0

        lax.fori_loop(0, window // rows, step, 0)


def attend_kernel(first_ref, low_ref, q_ref, k_ref, v_ref, o_ref, turned_ref, lse_ref, bias):
    rows, window = q_ref.shape[0], k_ref.shape[0]
    wide = QUERY_PER_KEY * rows
    fill_bias(low_ref, bias, rows, window)
    first = first_ref[0]
    for head in range(2):
        queries = three(q_ref, head, rows) * jnp.asarray(0.125, BF)
        lanes = slice(head * HEAD_WIDTH, (head + 1) * HEAD_WIDTH)

        def step(block, state):
            top, total, out = state
            span = pl.ds(pl.multiple_of(block * rows, rows), rows)
            shift = bias[span, :]
            scores = nt(k_ref[span, lanes], queries) + jnp.concatenate([shift] * QUERY_PER_KEY, 1)
            top_new = jnp.maximum(top, jnp.max(scores, axis=0, keepdims=True))
            weights = jnp.exp(scores - top_new)
            shrink = jnp.exp(top - top_new)
            total = total * shrink + jnp.sum(weights, axis=0, keepdims=True)
            out = out * shrink + tn(v_ref[span, lanes], weights.astype(BF))
            return (top_new, total, out)

        top, total, out = lax.fori_loop(
            first,
            window // rows,
            step,
            (
                jnp.full((1, wide), score_masked, F32),
                jnp.zeros((1, wide), F32),
                jnp.zeros((HEAD_WIDTH, wide), F32),
            ),
        )
        out = out / total
        turned_ref[head] = out
        lse_ref[head] = top + jnp.log(total)
        put_three(o_ref, head, rows, out)


def attend_grad_kernel(
    first_ref, low_ref, q_ref, k_ref, v_ref, do_ref, turned_ref, lse_ref, dq_ref, dk_ref, dv_ref, bias
):
    rows, window = q_ref.shape[0], k_ref.shape[0]
    wide = QUERY_PER_KEY * rows
    fill_bias(low_ref, bias, rows, window)
    first = first_ref[0]
    dk_ref[...] = jnp.zeros_like(dk_ref)
    dv_ref[...] = jnp.zeros_like(dv_ref)
    for head in range(2):
        queries = three(q_ref, head, rows) * jnp.asarray(0.125, BF)
        grads = three(do_ref, head, rows)
        delta = jnp.sum(grads.astype(F32).T * turned_ref[head], axis=0, keepdims=True)
        norm = lse_ref[head]
        lanes = slice(head * HEAD_WIDTH, (head + 1) * HEAD_WIDTH)

        def step(block, total):
            span = pl.ds(pl.multiple_of(block * rows, rows), rows)
            shift = bias[span, :]
            keys = k_ref[span, lanes]
            scores = nt(keys, queries) + jnp.concatenate([shift] * QUERY_PER_KEY, 1)
            weights = jnp.exp(scores - norm)
            prob_grad = nt(v_ref[span, lanes], grads)
            score_grad = (weights * (prob_grad - delta)).astype(BF)
            dv_ref[span, lanes] = nn(weights.astype(BF), grads).astype(BF)
            dk_ref[span, lanes] = nn(score_grad, queries).astype(BF)
            return total + tn(keys, score_grad)

        total = lax.fori_loop(first, window // rows, step, jnp.zeros((HEAD_WIDTH, wide), F32))
        put_three(dq_ref, head, rows, total * 0.125)


def attention_specs(rows, window):
    pair = 2 * QUERY_PER_KEY * HEAD_WIDTH
    pairs = KEY_HEADS // 2
    q_spec = pl.BlockSpec((rows, pair), lambda p: (0, p))
    k_spec = pl.BlockSpec((window, 2 * HEAD_WIDTH), lambda p: (0, p))
    v_spec = pl.BlockSpec((window, 2 * HEAD_WIDTH), lambda p: (0, p + pairs))
    turned = pl.BlockSpec((2, HEAD_WIDTH, QUERY_PER_KEY * rows), lambda p: (p, 0, 0))
    lse = pl.BlockSpec((2, 1, QUERY_PER_KEY * rows), lambda p: (p, 0, 0))
    first = pl.BlockSpec(memory_space=pltpu.SMEM)
    low = pl.BlockSpec((1, rows), lambda p: (0, 0))
    return pairs, q_spec, k_spec, v_spec, turned, lse, first, low


def attend(first, low, queries, keys_values):
    rows, window = queries.shape[0], keys_values.shape[0]
    pairs, q_spec, k_spec, v_spec, turned, lse, first_spec, low_spec = attention_specs(rows, window)
    wide = QUERY_PER_KEY * rows
    work = KEY_HEADS * wide * window
    return pl.pallas_call(
        attend_kernel,
        grid=(pairs,),
        in_specs=[first_spec, low_spec, q_spec, k_spec, v_spec],
        out_specs=[q_spec, turned, lse],
        out_shape=[
            jax.ShapeDtypeStruct((rows, QUERY_CHANNELS), BF),
            jax.ShapeDtypeStruct((KEY_HEADS, HEAD_WIDTH, wide), F32),
            jax.ShapeDtypeStruct((KEY_HEADS, 1, wide), F32),
        ],
        scratch_shapes=[pltpu.VMEM((window, rows), F32)],
        compiler_params=pltpu.CompilerParams(vmem_limit_bytes=40 << 20),
        cost_estimate=pl.CostEstimate(
            flops=4 * work * HEAD_WIDTH, transcendentals=work, bytes_accessed=8 << 20
        ),
        name="attend",
    )(first, low, queries, keys_values, keys_values)


def attend_grad(first, low, queries, keys_values, out_grad, turned_out, lse_rows):
    rows, window = queries.shape[0], keys_values.shape[0]
    pairs, q_spec, k_spec, v_spec, turned, lse, first_spec, low_spec = attention_specs(rows, window)
    wide = QUERY_PER_KEY * rows
    work = KEY_HEADS * wide * window
    return pl.pallas_call(
        attend_grad_kernel,
        grid=(pairs,),
        in_specs=[first_spec, low_spec, q_spec, k_spec, v_spec, q_spec, turned, lse],
        out_specs=[q_spec, k_spec, k_spec],
        out_shape=[
            jax.ShapeDtypeStruct((rows, QUERY_CHANNELS), BF),
            jax.ShapeDtypeStruct((window, KEY_CHANNELS), BF),
            jax.ShapeDtypeStruct((window, KEY_CHANNELS), BF),
        ],
        scratch_shapes=[pltpu.VMEM((window, rows), F32)],
        compiler_params=pltpu.CompilerParams(vmem_limit_bytes=40 << 20),
        cost_estimate=pl.CostEstimate(
            flops=10 * work * HEAD_WIDTH, transcendentals=work, bytes_accessed=12 << 20
        ),
        name="attend_grad",
    )(first, low, queries, keys_values, keys_values, out_grad, turned_out, lse_rows)


class Grid:
    def __init__(self, ctx, fsdp):
        self.ctx, self.fsdp = ctx, fsdp
        self.count = ctx * fsdp
        self.his = ctx // 2
        self.me = lax.axis_index("ctx") * fsdp + lax.axis_index("fsdp")
        self.lo = lax.rem(lax.axis_index("ctx"), 2)
        self.hi = lax.div(lax.axis_index("ctx"), 2)
        self.lo_mask = fsdp
        self.x_masks = []
        mask = fsdp // 2
        while mask > 1:
            self.x_masks.append(mask)
            mask //= 2

    def swap(self, value, mask):
        return lax.ppermute(value, AXES, [(i, i ^ mask) for i in range(self.count)])

    def shift_hi(self, value, by):
        step = by * 2 * self.fsdp
        pairs = [(i, i + step) for i in range(self.count) if 0 <= i + step < self.count]
        return lax.ppermute(value, AXES, pairs)

    def bit(self, mask):
        return lax.rem(lax.div(self.me, mask), 2)

    def ordered(self, own, got, mask):
        second = self.bit(mask) == 1
        return (jnp.where(second, got, own), jnp.where(second, own, got))

    def gather_rows(self, value, split):
        parts = [value] + [self.swap(value, m * 2 * self.fsdp) for m in range(1, self.his)]
        span = 1
        while span < self.his:
            odd = lax.rem(lax.div(self.hi, span), 2) == 1
            parts = [jnp.where(odd, parts[j ^ span], parts[j]) for j in range(self.his)]
            span *= 2
        held = jnp.stack(parts, axis=0)
        left, right = held[:, :, :split], held[:, :, split:]
        left = jnp.stack(self.ordered(left, self.swap(left, self.lo_mask), self.lo_mask), axis=1)
        for place, mask in enumerate(self.x_masks):
            axis = place + 1
            right = jnp.stack(self.ordered(right, self.swap(right, mask), mask), axis=axis)
            left = jnp.stack(self.ordered(left, self.swap(left, mask), mask), axis=axis + 1)
        right = jnp.stack(self.ordered(right, self.swap(right, self.lo_mask), self.lo_mask), axis=1)
        axis = left.ndim - 2
        left = jnp.stack(self.ordered(left, self.swap(left, 1), 1), axis=axis)
        right = jnp.stack(self.ordered(right, self.swap(right, 1), 1), axis=axis)
        return (left.reshape(-1, left.shape[-1]), right.reshape(-1, right.shape[-1]))

    def halve(self, value, axis, mask):
        mine = self.bit(mask)
        keep = lax.dynamic_index_in_dim(value, mine, axis, keepdims=False)
        send = lax.dynamic_index_in_dim(value, 1 - mine, axis, keepdims=False)
        got = self.swap(send.astype(BF), mask)
        return keep.astype(F32) + got.astype(F32)

    def scatter_rows(self, value, lo_first):
        bits = len(self.x_masks)
        rows = value.shape[0] // self.count
        value = value.reshape((self.his, 2) + (2,) * bits + (2, rows, value.shape[1]))
        value = self.halve(value, 2 + bits, 1)
        if lo_first:
            value = self.halve(value, 1, self.lo_mask)
        for mask in self.x_masks:
            value = self.halve(value, 1 if lo_first else 2, mask)
        if not lo_first:
            value = self.halve(value, 1, self.lo_mask)
        total = lax.dynamic_index_in_dim(value, self.hi, 0, keepdims=False).astype(F32)
        for m in range(1, self.his):
            other = jnp.bitwise_xor(self.hi, m)
            send = lax.dynamic_index_in_dim(value, other, 0, keepdims=False).astype(BF)
            total = total + self.swap(send, m * 2 * self.fsdp).astype(F32)
        return total

    def everyone(self, value):
        mask = 1
        while mask < self.count:
            value = value + self.swap(value, mask)
            mask *= 2
        return value


def per_device(
    ctx,
    fsdp,
    tokens,
    segment_ids,
    routes,
    upstream,
    step,
    qkv_weight,
    qkv_first,
    qkv_second,
    proj_weight,
    proj_first,
    proj_second,
    router_weight,
    router_first,
    router_second,
    norm_gains,
    gains_first,
    gains_second,
    gate_up,
    gate_up_first,
    gate_up_second,
    down_weight,
    down_first,
    down_second,
):
    grid = Grid(ctx, fsdp)
    rows = tokens.shape[1]
    width = tokens.shape[2]
    seq_len = segment_ids.shape[1]
    experts = router_weight.shape[1]
    capacity = 3 * rows // experts
    hops = (seq_len // 2) // (2 * rows)
    window = (2 * hops + 1) * rows
    groups = [[2 * h + l for h in range(grid.his)] for l in range(2)]
    owned = (qkv_weight, proj_weight, router_weight, norm_gains, gate_up, down_weight)
    step_counts = step.astype(F32)
    lo = grid.lo

    def pair_rows(shards):
        keep = lax.dynamic_index_in_dim(shards, lo, 0, keepdims=False)
        send = lax.dynamic_index_in_dim(shards, 1 - lo, 0, keepdims=False)
        both = grid.ordered(keep, grid.swap(send, grid.lo_mask), grid.lo_mask)
        return jnp.concatenate(both, axis=0)

    full_gate_up = lax.all_gather(
        pair_rows(gate_up), "ctx", axis=0, tiled=True, axis_index_groups=groups
    )
    full_down = lax.all_gather(
        pair_rows(down_weight), "ctx", axis=0, tiled=True, axis_index_groups=groups
    )

    own = tokens[0]
    chain = [own]
    for _ in range(hops):
        chain.append(grid.shift_hi(chain[-1], 1))
    blocks = [own]
    for k in range(1, hops + 1):
        blocks = [chain[k], grid.swap(jnp.where(lo == 0, chain[k - 1], chain[k]), grid.lo_mask)] + blocks
    seen = jnp.concatenate(blocks, axis=0)

    small = jnp.concatenate(
        [
            router_weight,
            norm_gains,
            jnp.zeros((router_weight.shape[0], 128 - experts - 2), BF),
        ],
        axis=1,
    )
    split = (QUERY_CHANNELS + 2 * KEY_CHANNELS) // 2
    qkv_left, qkv_right = grid.gather_rows(jnp.concatenate([qkv_weight, small], axis=1), split)
    full_small = qkv_right[:, split:]
    qkv_right = qkv_right[:, :split]
    full_router = full_small[:, :experts]
    full_gains = full_small[:, experts : experts + 2].astype(F32)
    attn_gain, moe_gain = full_gains[:, 0], full_gains[:, 1]
    half = QUERY_CHANNELS // 2
    proj_left, proj_right = grid.gather_rows(proj_weight, half)

    token_f = own.astype(F32)
    normed, norm_back = jax.vjp(rms_norm, token_f, attn_gain)
    hidden = normed.astype(BF)
    earlier_hidden = rms_norm(seen[: window - rows].astype(F32), attn_gain).astype(BF)
    hidden_window = jnp.concatenate([earlier_hidden, hidden], axis=0)
    rest = QUERY_CHANNELS - split
    queries = jnp.concatenate(
        [nn(hidden, qkv_left).astype(BF), nn(hidden, qkv_right[:, :rest]).astype(BF)], axis=1
    )
    keys_values = nn(hidden_window, qkv_right[:, rest:]).astype(BF)

    segments = segment_ids[0]
    start_own = lax.axis_index("ctx") * rows
    query_seg = lax.dynamic_slice_in_dim(segments, start_own, rows, 0)
    doc_start = jnp.sum((segments[None, :] < query_seg[:, None]).astype(jnp.int32), axis=1)
    low = (doc_start - start_own + (window - rows))[None, :]
    first = lax.div(jnp.maximum(low[0, :1], 0), rows)
    attended, turned_out, lse_rows = attend(first, low, queries, keys_values)

    branch = nt(attended[:, :half], proj_left) + nt(attended[:, half:], proj_right)
    middle = token_f + branch
    second_norm, second_back = jax.vjp(rms_norm, middle, moe_gain)
    second = second_norm.astype(BF)
    logits = nn(second, full_router)
    numbers = jnp.arange(experts, dtype=jnp.int32)
    chosen = routes[0][:, :, None] == numbers[None, None, :]
    combine, routing_back = jax.vjp(lambda values: routing(values, chosen), logits)

    partners = 2 * fsdp
    flat_routes = routes[0].reshape(-1)
    onehot = (flat_routes[:, None] == numbers[None, :]).astype(jnp.int32)
    earlier = jnp.cumsum(onehot, axis=0) - onehot
    slot_rank = jnp.sum(earlier * onehot, axis=1)
    home = lax.rem(flat_routes, 2) * fsdp + lax.div(flat_routes, 2)
    relative = jnp.bitwise_xor(home, lax.rem(grid.me, partners))
    positions = (relative * capacity + slot_rank).reshape(rows, 2)
    slots = experts * capacity
    slot_ids = jnp.arange(slots, dtype=jnp.int32)
    put = [(slot_ids[:, None] == positions[None, :, k]).astype(BF) for k in range(2)]
    put_both = put[0] + put[1]

    def exchange(sent):
        sent = sent.reshape(partners, capacity, width)
        return jnp.concatenate(
            [sent[0]] + [grid.swap(sent[m], m) for m in range(1, partners)], axis=0
        )

    grad_out = upstream[0].astype(F32)
    arrived = exchange(nn(put_both, second).astype(BF))
    scaled = [(combine[:, k : k + 1] * grad_out).astype(BF) for k in range(2)]
    back_arrived = exchange((nn(put[0], scaled[0]) + nn(put[1], scaled[1])).astype(BF))

    both_parts = nn(arrived, full_gate_up)
    gates = both_parts[:, :FF]
    ups = both_parts[:, FF:]
    sigmoid_gate = jax.nn.sigmoid(gates)
    silu_gate = gates * sigmoid_gate
    activated = (silu_gate * ups).astype(BF)
    returned = exchange(nn(activated, full_down).astype(BF))
    act_grad = nt(back_arrived, full_down)
    gate_grad = act_grad * ups * (sigmoid_gate + silu_gate * (1.0 - sigmoid_gate))
    up_grad = act_grad * silu_gate
    both_grad = jnp.concatenate([gate_grad, up_grad], axis=-1).astype(BF)
    back_returned = exchange(nt(both_grad, full_gate_up).astype(BF))

    def own_rows(full):
        part = lax.psum_scatter(
            full, "ctx", scatter_dimension=0, tiled=True, axis_index_groups=groups
        )
        part = part.reshape(2, part.shape[0] // 2, part.shape[1])
        keep = lax.dynamic_index_in_dim(part, lo, 0, keepdims=False)
        send = lax.dynamic_index_in_dim(part, 1 - lo, 0, keepdims=False)
        both = grid.ordered(keep, grid.swap(send, grid.lo_mask), grid.lo_mask)
        return jnp.stack(both, axis=0).astype(F32)

    down_grad = own_rows(tn(activated, back_arrived).astype(BF))
    gate_up_grad = own_rows(tn(arrived, both_grad).astype(BF))

    picked = [tn(put[k], returned) for k in range(2)]
    result = middle + combine[:, :1] * picked[0] + combine[:, 1:] * picked[1]
    block_out = result.astype(BF)[None]
    combine_grad = jnp.stack([jnp.sum(picked[k] * grad_out, axis=1) for k in range(2)], axis=1)
    copy_grads = tn(put_both, back_returned)
    (logit_grad,) = routing_back(combine_grad)
    router_f = full_router.astype(F32)
    second_grad = copy_grads + jnp.dot(
        logit_grad, router_f.T, precision=highest_mode, preferred_element_type=F32
    )
    router_full = jnp.dot(
        second.astype(F32).T, logit_grad, precision=highest_mode, preferred_element_type=F32
    )
    middle_norm_grad, moe_gain_grad = second_back(second_grad)
    middle_grad = grad_out + middle_norm_grad
    middle_low = middle_grad.astype(BF)
    out_grad = jnp.concatenate(
        [nn(middle_low, proj_left).astype(BF), nn(middle_low, proj_right).astype(BF)], axis=1
    )
    proj_full = tn(middle_low, attended).astype(BF)
    side = jnp.concatenate(
        [
            router_full.astype(BF),
            moe_gain_grad[:, None].astype(BF),
            jnp.zeros((width, 128 - experts - 1), BF),
        ],
        axis=1,
    )
    proj_grad_left = grid.scatter_rows(proj_full[:, :half], False)
    proj_grad_right = grid.scatter_rows(jnp.concatenate([proj_full[:, half:], side], axis=1), True)
    proj_grad = jnp.concatenate([proj_grad_left, proj_grad_right[:, :half]], axis=1)
    router_grad = proj_grad_right[:, half : half + experts]
    moe_own = proj_grad_right[:, half + experts]

    query_grad, key_part, value_part = attend_grad(
        first, low, queries, keys_values, out_grad, turned_out, lse_rows
    )
    kv_part = jnp.concatenate([key_part, value_part], axis=1)
    qkv_full = jnp.concatenate(
        [tn(hidden, query_grad).astype(BF), tn(hidden_window, kv_part).astype(BF)], axis=1
    )
    qkv_grad = jnp.concatenate(
        [
            grid.scatter_rows(qkv_full[:, :split], False),
            grid.scatter_rows(qkv_full[:, split:], True),
        ],
        axis=1,
    )

    parts = [kv_part[j * rows : (j + 1) * rows] for j in range(2 * hops + 1)]
    crossed = [None] + [parts[2 * (hops - k) + 1] for k in range(1, hops + 1)]
    kept = [parts[2 * hops]] + [parts[2 * (hops - k)] for k in range(1, hops + 1)]
    got = [None] + [grid.swap(crossed[k], grid.lo_mask) for k in range(1, hops + 1)]
    sums = []
    for k in range(hops + 1):
        after = got[k + 1].astype(F32) if k < hops else 0.0
        here = got[k].astype(F32) if k > 0 else 0.0
        sums.append(kept[k].astype(F32) + jnp.where(lo == 1, here, after))
    running = sums[hops]
    for k in range(hops, 0, -1):
        running = sums[k - 1] + grid.shift_hi(running.astype(BF), -1).astype(F32)
    kv_grad = running.astype(BF)

    hidden_grad = (
        nt(query_grad[:, :split], qkv_left)
        + nt(query_grad[:, split:], qkv_right[:, :rest])
        + nt(kv_grad, qkv_right[:, rest:])
    )
    token_norm_grad, attn_gain_grad = norm_back(hidden_grad)
    token_grad = (middle_grad + token_norm_grad)[None]
    attn_sum = grid.everyone(attn_gain_grad.reshape(-1, 128))
    attn_own = lax.dynamic_index_in_dim(attn_sum.reshape(grid.count, -1), grid.me, 0, keepdims=False)
    gains_grad = jnp.stack([attn_own, moe_own], axis=1)

    gradients = (qkv_grad, proj_grad, router_grad, gains_grad, gate_up_grad, down_grad)
    firsts = (qkv_first, proj_first, router_first, gains_first, gate_up_first, down_first)
    seconds = (qkv_second, proj_second, router_second, gains_second, gate_up_second, down_second)
    states = [
        adam_ratio(
            owned[number], gradients[number], firsts[number], seconds[number], step_counts[number]
        )
        for number in range(6)
    ]
    weight_sq = jnp.stack([jnp.sum(jnp.square(tensor.astype(F32))) for tensor in owned])
    ratio_sq = jnp.stack([jnp.sum(entry[2] * entry[2]) for entry in states])
    sums_all = grid.everyone(jnp.stack([weight_sq, ratio_sq]))
    weight_tot, ratio_tot = sums_all[0], sums_all[1]
    trust_ratio = jnp.sqrt(weight_tot) * lax.rsqrt(ratio_tot + ratio_epsilon)
    new_weights = [
        owned[number].astype(F32) - learn_rate * trust_ratio[number] * states[number][2]
        for number in range(6)
    ]
    matrix_norms = 0.5 * jnp.log(jnp.stack([weight_tot, ratio_tot + ratio_epsilon]))
    return (
        block_out,
        token_grad,
        *gradients,
        *[entry[0] for entry in states],
        *[entry[1] for entry in states],
        *new_weights,
        matrix_norms,
    )


def solution(mesh):
    rows = P(("ctx", "fsdp"), None)
    tokens = P("fsdp", "ctx", None)
    weights = [rows] * 4 + [tokens] * 2
    return jax.shard_map(
        functools.partial(per_device, mesh.shape["ctx"], mesh.shape["fsdp"]),
        mesh=mesh,
        in_specs=(tokens, P("fsdp", None), tokens, tokens, P())
        + tuple(spec for spec in weights for _ in range(3)),
        out_specs=(tokens, tokens) + tuple(weights) * 4 + (P(),),
        check_vma=False,
    )
```

```python
import functools

import jax
import jax.numpy as jnp
from jax import lax
from jax.experimental import pallas as pl
from jax.experimental.pallas import tpu as pltpu
from jax.sharding import PartitionSpec as P

KEY_HEADS = 8
HEAD_WIDTH = 64
FF = 1024
QUERY_PER_KEY = 3
QUERY_CHANNELS = 1536
KEY_CHANNELS = 512

norm_epsilon = 1e-05
beta_first = 0.9
beta_second = 0.99
adam_epsilon = 1e-08
weight_decay = 0.01
learn_rate = 0.5
ratio_epsilon = 1e-06
score_masked = -1e30
highest_mode = lax.Precision.HIGHEST


BF = jnp.bfloat16
F32 = jnp.float32
AXES = ("ctx", "fsdp")


def rms_norm(values, gain_vec):
    scaling = lax.rsqrt(jnp.mean(values * values, axis=-1, keepdims=True) + norm_epsilon)
    return values * scaling * gain_vec


def routing(logits, chosen):
    probabilities = jax.nn.softmax(logits, axis=-1)
    picked = jnp.sum(jnp.where(chosen, probabilities[:, None, :], 0.0), axis=2)
    return picked / jnp.sum(picked, axis=1, keepdims=True)


def adam_ratio(weight, gradient, first_old, second_old, step_count):
    tensor = weight.astype(F32)
    bias_one = 1.0 - jnp.power(beta_first, step_count)
    bias_two = 1.0 - jnp.power(beta_second, step_count)
    first_new = beta_first * first_old + (1.0 - beta_first) * gradient
    second_new = beta_second * second_old + (1.0 - beta_second) * gradient * gradient
    step_ratio = (
        first_new / bias_one / (jnp.sqrt(second_new / bias_two) + adam_epsilon)
        + weight_decay * tensor
    )
    return (first_new, second_new, step_ratio)


def nt(left, right):
    return lax.dot_general(left, right, (((1,), (1,)), ((), ())), preferred_element_type=F32)


def tn(left, right):
    return lax.dot_general(left, right, (((0,), (0,)), ((), ())), preferred_element_type=F32)


def nn(left, right):
    return jnp.dot(left, right, preferred_element_type=F32)


def tie(value, *others):
    return lax.optimization_barrier((value, *others))[0]


def three_parts(value):
    high = lax.reduce_precision(value, 8, 7)
    rest = value - high
    middle = lax.reduce_precision(rest, 8, 7)
    parts = jnp.concatenate([high, middle, rest - middle], axis=1).astype(BF)
    return jnp.pad(parts, ((0, 0), (0, 125)))


def three(ref, head, rows):
    base = head * QUERY_PER_KEY * HEAD_WIDTH
    return jnp.concatenate(
        [
            ref[:, base + g * HEAD_WIDTH : base + (g + 1) * HEAD_WIDTH]
            for g in range(QUERY_PER_KEY)
        ],
        axis=0,
    )


def put_three(ref, head, rows, turned):
    base = head * QUERY_PER_KEY * HEAD_WIDTH
    for g in range(QUERY_PER_KEY):
        part = turned[:, g * rows : (g + 1) * rows]
        ref[:, base + g * HEAD_WIDTH : base + (g + 1) * HEAD_WIDTH] = part.T.astype(ref.dtype)


def fill_bias(low_ref, bias, rows, window):
    @pl.when(pl.program_id(0) == 0)
    def _():
        def step(block, _):
            start = pl.multiple_of(block * rows, rows)
            key_pos = start + lax.broadcasted_iota(jnp.int32, (rows, rows), 0)
            top = lax.broadcasted_iota(jnp.int32, (rows, rows), 1) + (window - rows)
            allowed = (key_pos >= low_ref[...]) & (key_pos <= top)
            bias[pl.ds(start, rows), :] = jnp.where(allowed, 0.0, score_masked)
            return 0

        lax.fori_loop(0, window // rows, step, 0)


def attend_kernel(first_ref, low_ref, q_ref, k_ref, v_ref, o_ref, turned_ref, lse_ref, bias):
    rows, window = q_ref.shape[0], k_ref.shape[0]
    wide = QUERY_PER_KEY * rows
    fill_bias(low_ref, bias, rows, window)
    first = first_ref[0]
    for head in range(2):
        queries = three(q_ref, head, rows) * jnp.asarray(0.125, BF)
        lanes = slice(head * HEAD_WIDTH, (head + 1) * HEAD_WIDTH)

        def step(block, state):
            top, total, out = state
            span = pl.ds(pl.multiple_of(block * rows, rows), rows)
            shift = bias[span, :]
            scores = nt(k_ref[span, lanes], queries) + jnp.concatenate([shift] * QUERY_PER_KEY, 1)
            top_new = jnp.maximum(top, jnp.max(scores, axis=0, keepdims=True))
            weights = jnp.exp(scores - top_new)
            shrink = jnp.exp(top - top_new)
            total = total * shrink + jnp.sum(weights, axis=0, keepdims=True)
            out = out * shrink + tn(v_ref[span, lanes], weights.astype(BF))
            return (top_new, total, out)

        top, total, out = lax.fori_loop(
            first,
            window // rows,
            step,
            (
                jnp.full((1, wide), score_masked, F32),
                jnp.zeros((1, wide), F32),
                jnp.zeros((HEAD_WIDTH, wide), F32),
            ),
        )
        out = out / total
        turned_ref[head] = out
        lse_ref[head] = top + jnp.log(total)
        put_three(o_ref, head, rows, out)


def attend_grad_kernel(
    first_ref, low_ref, q_ref, k_ref, v_ref, do_ref, turned_ref, lse_ref, dq_ref, dk_ref, dv_ref, bias
):
    rows, window = q_ref.shape[0], k_ref.shape[0]
    wide = QUERY_PER_KEY * rows
    fill_bias(low_ref, bias, rows, window)
    first = first_ref[0]
    dk_ref[...] = jnp.zeros_like(dk_ref)
    dv_ref[...] = jnp.zeros_like(dv_ref)
    for head in range(2):
        queries = three(q_ref, head, rows) * jnp.asarray(0.125, BF)
        grads = three(do_ref, head, rows)
        delta = jnp.sum(grads.astype(F32).T * turned_ref[head], axis=0, keepdims=True)
        norm = lse_ref[head]
        lanes = slice(head * HEAD_WIDTH, (head + 1) * HEAD_WIDTH)

        def step(block, total):
            span = pl.ds(pl.multiple_of(block * rows, rows), rows)
            shift = bias[span, :]
            keys = k_ref[span, lanes]
            scores = nt(keys, queries) + jnp.concatenate([shift] * QUERY_PER_KEY, 1)
            weights = jnp.exp(scores - norm)
            prob_grad = nt(v_ref[span, lanes], grads)
            score_grad = (weights * (prob_grad - delta)).astype(BF)
            dv_ref[span, lanes] = nn(weights.astype(BF), grads).astype(BF)
            dk_ref[span, lanes] = nn(score_grad, queries).astype(BF)
            return total + tn(keys, score_grad)

        total = lax.fori_loop(first, window // rows, step, jnp.zeros((HEAD_WIDTH, wide), F32))
        put_three(dq_ref, head, rows, total * 0.125)


def attention_specs(rows, window):
    pair = 2 * QUERY_PER_KEY * HEAD_WIDTH
    pairs = KEY_HEADS // 2
    q_spec = pl.BlockSpec((rows, pair), lambda p: (0, p))
    k_spec = pl.BlockSpec((window, 2 * HEAD_WIDTH), lambda p: (0, p))
    v_spec = pl.BlockSpec((window, 2 * HEAD_WIDTH), lambda p: (0, p + pairs))
    turned = pl.BlockSpec((2, HEAD_WIDTH, QUERY_PER_KEY * rows), lambda p: (p, 0, 0))
    lse = pl.BlockSpec((2, 1, QUERY_PER_KEY * rows), lambda p: (p, 0, 0))
    first = pl.BlockSpec(memory_space=pltpu.SMEM)
    low = pl.BlockSpec((1, rows), lambda p: (0, 0))
    return pairs, q_spec, k_spec, v_spec, turned, lse, first, low


def attend(first, low, queries, keys_values):
    rows, window = queries.shape[0], keys_values.shape[0]
    pairs, q_spec, k_spec, v_spec, turned, lse, first_spec, low_spec = attention_specs(rows, window)
    wide = QUERY_PER_KEY * rows
    work = KEY_HEADS * wide * window
    return pl.pallas_call(
        attend_kernel,
        grid=(pairs,),
        in_specs=[first_spec, low_spec, q_spec, k_spec, v_spec],
        out_specs=[q_spec, turned, lse],
        out_shape=[
            jax.ShapeDtypeStruct((rows, QUERY_CHANNELS), BF),
            jax.ShapeDtypeStruct((KEY_HEADS, HEAD_WIDTH, wide), F32),
            jax.ShapeDtypeStruct((KEY_HEADS, 1, wide), F32),
        ],
        scratch_shapes=[pltpu.VMEM((window, rows), F32)],
        compiler_params=pltpu.CompilerParams(vmem_limit_bytes=40 << 20),
        cost_estimate=pl.CostEstimate(
            flops=4 * work * HEAD_WIDTH, transcendentals=work, bytes_accessed=8 << 20
        ),
        name="attend",
    )(first, low, queries, keys_values, keys_values)


def attend_grad(first, low, queries, keys_values, out_grad, turned_out, lse_rows):
    rows, window = queries.shape[0], keys_values.shape[0]
    pairs, q_spec, k_spec, v_spec, turned, lse, first_spec, low_spec = attention_specs(rows, window)
    wide = QUERY_PER_KEY * rows
    work = KEY_HEADS * wide * window
    return pl.pallas_call(
        attend_grad_kernel,
        grid=(pairs,),
        in_specs=[first_spec, low_spec, q_spec, k_spec, v_spec, q_spec, turned, lse],
        out_specs=[q_spec, k_spec, k_spec],
        out_shape=[
            jax.ShapeDtypeStruct((rows, QUERY_CHANNELS), BF),
            jax.ShapeDtypeStruct((window, KEY_CHANNELS), BF),
            jax.ShapeDtypeStruct((window, KEY_CHANNELS), BF),
        ],
        scratch_shapes=[pltpu.VMEM((window, rows), F32)],
        compiler_params=pltpu.CompilerParams(vmem_limit_bytes=40 << 20),
        cost_estimate=pl.CostEstimate(
            flops=10 * work * HEAD_WIDTH, transcendentals=work, bytes_accessed=12 << 20
        ),
        name="attend_grad",
    )(first, low, queries, keys_values, keys_values, out_grad, turned_out, lse_rows)


class Grid:
    def __init__(self, ctx, fsdp):
        self.ctx, self.fsdp = ctx, fsdp
        self.count = ctx * fsdp
        self.his = ctx // 2
        self.me = lax.axis_index("ctx") * fsdp + lax.axis_index("fsdp")
        self.lo = lax.rem(lax.axis_index("ctx"), 2)
        self.hi = lax.div(lax.axis_index("ctx"), 2)
        self.lo_mask = fsdp
        self.x_masks = []
        mask = fsdp // 2
        while mask > 1:
            self.x_masks.append(mask)
            mask //= 2

    def swap(self, value, mask):
        return lax.ppermute(value, AXES, [(i, i ^ mask) for i in range(self.count)])

    def shift_hi(self, value, by):
        step = by * 2 * self.fsdp
        pairs = [(i, i + step) for i in range(self.count) if 0 <= i + step < self.count]
        return lax.ppermute(value, AXES, pairs)

    def bit(self, mask):
        return lax.rem(lax.div(self.me, mask), 2)

    def ordered(self, own, got, mask):
        second = self.bit(mask) == 1
        return (jnp.where(second, got, own), jnp.where(second, own, got))

    def gather_hi(self, value):
        return [self.swap(value, m * 2 * self.fsdp) for m in range(1, self.his)]

    def order_hi(self, own, got):
        parts = [own] + got
        span = 1
        while span < self.his:
            odd = lax.rem(lax.div(self.hi, span), 2) == 1
            parts = [jnp.where(odd, parts[j ^ span], parts[j]) for j in range(self.his)]
            span *= 2
        return jnp.stack(parts, axis=0)

    def join(self, value, mask, axis, last=None):
        got = self.swap(value, mask)
        if last is not None:
            got = tie(got, last)
        return jnp.stack(self.ordered(value, got, mask), axis=axis)

    def gather_one(self, held, split):
        left, right = held[:, :, :split], held[:, :, split:]
        left = self.join(left, self.lo_mask, 1)
        for place, mask in enumerate(self.x_masks):
            right = self.join(right, mask, place + 1)
        return left, right

    def gather_two(self, left, right, last=None):
        for place, mask in enumerate(self.x_masks):
            left = self.join(left, mask, place + 2, last)
        return left, self.join(right, self.lo_mask, 1, last)

    def gather_core(self, value):
        value = jnp.stack(self.ordered(value, self.swap(value, 1), 1), axis=value.ndim - 2)
        return value.reshape(-1, value.shape[-1])

    def halve(self, value, axis, mask):
        mine = self.bit(mask)
        keep = lax.dynamic_index_in_dim(value, mine, axis, keepdims=False)
        send = lax.dynamic_index_in_dim(value, 1 - mine, axis, keepdims=False)
        got = self.swap(send.astype(BF), mask)
        return keep.astype(F32) + got.astype(F32)

    def scatter_core(self, value):
        bits = len(self.x_masks)
        rows = value.shape[0] // self.count
        value = value.reshape((self.his, 2) + (2,) * bits + (2, rows, value.shape[1]))
        return self.halve(value, 2 + bits, 1)

    def scatter_lo(self, value):
        return self.halve(value, 1, self.lo_mask)

    def scatter_x(self, value, after_lo):
        for mask in self.x_masks:
            value = self.halve(value, 1 if after_lo else 2, mask)
        return value

    def scatter_hi(self, value):
        total = lax.dynamic_index_in_dim(value, self.hi, 0, keepdims=False).astype(F32)
        for m in range(1, self.his):
            other = jnp.bitwise_xor(self.hi, m)
            send = lax.dynamic_index_in_dim(value, other, 0, keepdims=False).astype(BF)
            total = total + self.swap(send, m * 2 * self.fsdp).astype(F32)
        return total

    def everyone(self, value):
        mask = 1
        while mask < self.count:
            value = value + self.swap(value, mask)
            mask *= 2
        return value


def per_device(
    ctx,
    fsdp,
    tokens,
    segment_ids,
    routes,
    upstream,
    step,
    qkv_weight,
    qkv_first,
    qkv_second,
    proj_weight,
    proj_first,
    proj_second,
    router_weight,
    router_first,
    router_second,
    norm_gains,
    gains_first,
    gains_second,
    gate_up,
    gate_up_first,
    gate_up_second,
    down_weight,
    down_first,
    down_second,
):
    grid = Grid(ctx, fsdp)
    rows = tokens.shape[1]
    width = tokens.shape[2]
    seq_len = segment_ids.shape[1]
    experts = router_weight.shape[1]
    capacity = 3 * rows // experts
    hops = (seq_len // 2) // (2 * rows)
    window = (2 * hops + 1) * rows
    groups = [[2 * h + l for h in range(grid.his)] for l in range(2)]
    owned = (qkv_weight, proj_weight, router_weight, norm_gains, gate_up, down_weight)
    step_counts = step.astype(F32)
    lo = grid.lo

    def mine(shards):
        return lax.dynamic_index_in_dim(shards, lo, 0, keepdims=False)

    def others(shards):
        return lax.dynamic_index_in_dim(shards, 1 - lo, 0, keepdims=False)

    def cross(value):
        return grid.swap(value, grid.lo_mask)

    def both_rows(keep, got):
        return jnp.concatenate(grid.ordered(keep, got, grid.lo_mask), axis=0)

    def gather_experts(pair):
        return lax.all_gather(pair, "ctx", axis=0, tiled=True, axis_index_groups=groups)

    small = jnp.concatenate(
        [
            router_weight,
            norm_gains,
            jnp.zeros((router_weight.shape[0], 128 - experts - 2), BF),
        ],
        axis=1,
    )
    split = QUERY_CHANNELS
    half = QUERY_CHANNELS // 2
    qkv_own = jnp.concatenate([qkv_weight, small], axis=1)
    qkv_got = grid.gather_hi(qkv_own)
    own = tokens[0]
    chain = [own, grid.shift_hi(tie(own, qkv_got[0], qkv_got[-1]), 1)]
    gate_up_got = cross(others(gate_up))

    for _ in range(1, hops):
        chain.append(grid.shift_hi(chain[-1], 1))
    across = [cross(jnp.where(lo == 0, chain[k - 1], chain[k])) for k in range(1, hops + 1)]
    qkv_left, qkv_right = grid.gather_one(grid.order_hi(qkv_own, qkv_got), split)
    proj_got = grid.gather_hi(tie(proj_weight, qkv_got[0], qkv_got[-1]))

    gate_up_pair = both_rows(mine(gate_up), gate_up_got)
    full_gate_up = gather_experts(tie(gate_up_pair, chain[hops], qkv_left, qkv_right, *proj_got))
    down_got = cross(tie(others(down_weight), across[hops - 1]))
    full_down = gather_experts(both_rows(mine(down_weight), down_got))

    qkv_left, qkv_right = grid.gather_two(qkv_left, qkv_right)
    proj_held = tie(grid.order_hi(proj_weight, proj_got), qkv_left, qkv_right)
    proj_left, proj_right = grid.gather_one(proj_held, half)

    numbers = jnp.arange(experts, dtype=jnp.int32)
    chosen = routes[0][:, :, None] == numbers[None, None, :]
    partners = 2 * fsdp
    flat_routes = routes[0].reshape(-1)
    onehot = (flat_routes[:, None] == numbers[None, :]).astype(jnp.int32)
    earlier = jnp.cumsum(onehot, axis=0) - onehot
    slot_rank = jnp.sum(earlier * onehot, axis=1)
    home = lax.rem(flat_routes, 2) * fsdp + lax.div(flat_routes, 2)
    relative = jnp.bitwise_xor(home, lax.rem(grid.me, partners))
    positions = (relative * capacity + slot_rank).reshape(rows, 2)
    slots = experts * capacity
    slot_ids = jnp.arange(slots, dtype=jnp.int32)
    put = [(slot_ids[:, None] == positions[None, :, k]).astype(BF) for k in range(2)]
    put_both = put[0] + put[1]
    put_wide = jnp.concatenate(put, axis=1)

    def exchange(sent):
        sent = sent.reshape(partners, capacity, sent.shape[1])
        return [sent[0]] + [grid.swap(sent[m], m) for m in range(1, partners)]

    def rows_of(pieces):
        return jnp.concatenate([piece[:, :width] for piece in pieces], axis=0)

    def sides_of(pieces):
        return jnp.concatenate([piece[:, width:] for piece in pieces], axis=0)

    qkv_left = grid.gather_core(qkv_left)
    qkv_right = grid.gather_core(qkv_right)
    full_small = qkv_right[:, 2 * KEY_CHANNELS :]
    qkv_right = qkv_right[:, : 2 * KEY_CHANNELS]
    full_router = full_small[:, :experts]
    full_gains = full_small[:, experts : experts + 2].astype(F32)
    attn_gain, moe_gain = full_gains[:, 0], full_gains[:, 1]

    blocks = [own]
    for k in range(1, hops + 1):
        blocks = [chain[k], across[k - 1]] + blocks
    token_f = own.astype(F32)
    normed, norm_back = jax.vjp(rms_norm, token_f, attn_gain)
    hidden = normed.astype(BF)
    seen = jnp.concatenate(blocks[:-1], axis=0)
    earlier_hidden = rms_norm(seen.astype(F32), attn_gain).astype(BF)
    hidden_window = jnp.concatenate([earlier_hidden, hidden], axis=0)
    queries = nn(hidden, qkv_left).astype(BF)
    keys_values = nn(hidden_window, qkv_right).astype(BF)
    proj_left, proj_right = grid.gather_two(proj_left, proj_right, keys_values)
    proj_left = grid.gather_core(proj_left)
    proj_right = grid.gather_core(proj_right)
    upstream_held = tie(upstream[0], keys_values)
    dy_pieces = exchange(nn(put_both, upstream_held).astype(BF))

    segments = segment_ids[0]
    start_own = lax.axis_index("ctx") * rows
    query_seg = lax.dynamic_slice_in_dim(segments, start_own, rows, 0)
    doc_start = jnp.sum((segments[None, :] < query_seg[:, None]).astype(jnp.int32), axis=1)
    low = (doc_start - start_own + (window - rows))[None, :]
    first = lax.div(jnp.maximum(low[0, :1], 0), rows)
    attended, turned_out, lse_rows = attend(first, low, queries, keys_values)

    dy_rows = jnp.concatenate([tie(piece, attended) for piece in dy_pieces], axis=0)
    branch = nt(attended[:, :half], proj_left) + nt(attended[:, half:], proj_right)
    middle = token_f + branch
    second_norm, second_back = jax.vjp(rms_norm, middle, moe_gain)
    second = second_norm.astype(BF)
    logits = nn(second, full_router)
    combine, routing_back = jax.vjp(lambda values: routing(values, chosen), logits)
    wide_rows = jnp.concatenate(
        [
            jnp.concatenate([second, three_parts(combine[:, k : k + 1])], axis=1)
            for k in range(2)
        ],
        axis=0,
    )
    arrived_pieces = exchange(nn(put_wide, wide_rows).astype(BF))
    arrived = rows_of(arrived_pieces)
    shares = jnp.sum(sides_of(arrived_pieces).astype(F32), axis=1, keepdims=True)
    back_arrived = (shares * dy_rows.astype(F32)).astype(BF)

    both_parts = nn(arrived, full_gate_up)
    gates = both_parts[:, :FF]
    ups = both_parts[:, FF:]
    sigmoid_gate = jax.nn.sigmoid(gates)
    silu_gate = gates * sigmoid_gate
    activated = lax.optimization_barrier((silu_gate * ups).astype(BF))

    def reduce_experts(full):
        return lax.psum_scatter(
            full, "ctx", scatter_dimension=0, tiled=True, axis_index_groups=groups
        )

    def own_rows(part):
        part = part.reshape(2, part.shape[0] // 2, part.shape[1])
        both = grid.ordered(mine(part), cross(others(part)), grid.lo_mask)
        return jnp.stack(both, axis=0).astype(F32)

    down_full = tn(activated, back_arrived).astype(BF)
    down_part = reduce_experts(down_full)
    full_down = tie(full_down, down_full)
    act_grad = nt(back_arrived, full_down)
    gate_grad = act_grad * ups * (sigmoid_gate + silu_gate * (1.0 - sigmoid_gate))
    up_grad = act_grad * silu_gate
    both_grad = jnp.concatenate([gate_grad, up_grad], axis=-1).astype(BF)
    produced = nn(activated, full_down).astype(BF)
    share_grads = jnp.sum(produced.astype(F32) * dy_rows.astype(F32), axis=1, keepdims=True)
    row_grads = jnp.concatenate(
        [nt(both_grad, full_gate_up).astype(BF), three_parts(share_grads)], axis=1
    )
    back_pieces = exchange(row_grads)
    gate_up_full = tn(arrived, tie(both_grad, row_grads)).astype(BF)
    gate_up_part = reduce_experts(gate_up_full)
    back_pieces = [tie(piece, gate_up_full) for piece in back_pieces]
    back_returned = rows_of(back_pieces)
    back_sides = sides_of(back_pieces)

    grad_out = upstream[0].astype(F32)
    combine_grad = jnp.stack(
        [jnp.sum(tn(put[k], back_sides), axis=1) for k in range(2)], axis=1
    )
    copy_grads = tn(put_both, back_returned)
    (logit_grad,) = routing_back(combine_grad)
    router_f = full_router.astype(F32)
    second_grad = copy_grads + jnp.dot(
        logit_grad, router_f.T, precision=highest_mode, preferred_element_type=F32
    )
    router_full = jnp.dot(
        second.astype(F32).T, logit_grad, precision=highest_mode, preferred_element_type=F32
    )
    middle_norm_grad, moe_gain_grad = second_back(second_grad)
    middle_grad = grad_out + middle_norm_grad
    middle_low = middle_grad.astype(BF)
    out_grad = jnp.concatenate(
        [nn(middle_low, proj_left).astype(BF), nn(middle_low, proj_right).astype(BF)], axis=1
    )
    proj_one = tn(middle_low, attended[:, :half]).astype(BF)
    proj_two = tn(middle_low, attended[:, half:]).astype(BF)
    side = jnp.concatenate(
        [
            router_full.astype(BF),
            moe_gain_grad[:, None].astype(BF),
            jnp.zeros((width, 128 - experts - 1), BF),
        ],
        axis=1,
    )
    out_grad = tie(out_grad, proj_one, proj_two)
    proj_one = grid.scatter_core(proj_one)
    proj_two = grid.scatter_core(jnp.concatenate([proj_two, side], axis=1))

    query_grad, key_part, value_part = attend_grad(
        first, low, queries, keys_values, out_grad, turned_out, lse_rows
    )
    kv_part = jnp.concatenate([key_part, value_part], axis=1)
    qkv_one = grid.scatter_core(tn(hidden, query_grad).astype(BF))
    qkv_two = grid.scatter_core(tn(hidden_window, kv_part).astype(BF))
    proj_one = grid.scatter_x(proj_one, False)
    proj_two = grid.scatter_lo(proj_two)

    parts = [kv_part[j * rows : (j + 1) * rows] for j in range(2 * hops + 1)]
    crossed = [None] + [parts[2 * (hops - k) + 1] for k in range(1, hops + 1)]
    kept = [parts[2 * hops]] + [parts[2 * (hops - k)] for k in range(1, hops + 1)]
    got = [None] + [cross(crossed[k]) for k in range(1, hops + 1)]
    sums = []
    for k in range(hops + 1):
        after = got[k + 1].astype(F32) if k < hops else 0.0
        here = got[k].astype(F32) if k > 0 else 0.0
        sums.append(kept[k].astype(F32) + jnp.where(lo == 1, here, after))

    qkv_core = qkv_one
    qkv_one = grid.scatter_x(qkv_one, False)
    qkv_two = grid.scatter_lo(qkv_two)
    proj_one = grid.scatter_lo(proj_one)
    proj_two = grid.scatter_x(proj_two, True)
    qkv_stage = qkv_core
    qkv_one = grid.scatter_lo(qkv_one)
    qkv_two = grid.scatter_x(qkv_two, True)
    running = tie(sums[hops], qkv_stage)
    for k in range(hops, 0, -1):
        running = sums[k - 1] + grid.shift_hi(running.astype(BF), -1).astype(F32)
        running = tie(running, qkv_one, qkv_two)
    kv_grad = running.astype(BF)
    down_grad = own_rows(down_part)
    qkv_grad = jnp.concatenate([grid.scatter_hi(qkv_one), grid.scatter_hi(qkv_two)], axis=1)
    proj_left_grad, proj_right_grad = [
        grid.scatter_hi(tie(part, qkv_one, qkv_two)) for part in (proj_one, proj_two)
    ]
    proj_grad = jnp.concatenate([proj_left_grad, proj_right_grad[:, :half]], axis=1)
    router_grad = proj_right_grad[:, half : half + experts]
    moe_own = proj_right_grad[:, half + experts]
    gate_up_grad = own_rows(tie(gate_up_part, down_grad))

    query_after = tie(query_grad, qkv_core)
    hidden_grad = (
        nt(query_after, qkv_left) + nt(kv_grad, qkv_right)
    )
    token_norm_grad, attn_gain_grad = norm_back(hidden_grad)
    token_grad = (middle_grad + token_norm_grad)[None]
    attn_sum = grid.everyone(attn_gain_grad.reshape(-1, 128))
    attn_own = lax.dynamic_index_in_dim(attn_sum.reshape(grid.count, -1), grid.me, 0, keepdims=False)
    gains_grad = jnp.stack([attn_own, moe_own], axis=1)

    returned = jnp.concatenate(exchange(tie(produced, qkv_one, qkv_two)), axis=0)
    picked = [tn(put[k], returned) for k in range(2)]
    result = middle + combine[:, :1] * picked[0] + combine[:, 1:] * picked[1]
    block_out = result.astype(BF)[None]

    gradients = (qkv_grad, proj_grad, router_grad, gains_grad, gate_up_grad, down_grad)
    firsts = (qkv_first, proj_first, router_first, gains_first, gate_up_first, down_first)
    seconds = (qkv_second, proj_second, router_second, gains_second, gate_up_second, down_second)
    states = [
        adam_ratio(
            owned[number], gradients[number], firsts[number], seconds[number], step_counts[number]
        )
        for number in range(6)
    ]
    weight_sq = jnp.stack([jnp.sum(jnp.square(tensor.astype(F32))) for tensor in owned])
    ratio_sq = jnp.stack([jnp.sum(entry[2] * entry[2]) for entry in states])
    sums_all = grid.everyone(jnp.stack([weight_sq, ratio_sq]))
    weight_tot, ratio_tot = sums_all[0], sums_all[1]
    trust_ratio = jnp.sqrt(weight_tot) * lax.rsqrt(ratio_tot + ratio_epsilon)
    new_weights = [
        owned[number].astype(F32) - learn_rate * trust_ratio[number] * states[number][2]
        for number in range(6)
    ]
    matrix_norms = 0.5 * jnp.log(jnp.stack([weight_tot, ratio_tot + ratio_epsilon]))
    return (
        block_out,
        token_grad,
        *gradients,
        *[entry[0] for entry in states],
        *[entry[1] for entry in states],
        *new_weights,
        matrix_norms,
    )


def solution(mesh):
    rows = P(("ctx", "fsdp"), None)
    tokens = P("fsdp", "ctx", None)
    weights = [rows] * 4 + [tokens] * 2
    return jax.shard_map(
        functools.partial(per_device, mesh.shape["ctx"], mesh.shape["fsdp"]),
        mesh=mesh,
        in_specs=(tokens, P("fsdp", None), tokens, tokens, P())
        + tuple(spec for spec in weights for _ in range(3)),
        out_specs=(tokens, tokens) + tuple(weights) * 4 + (P(),),
        check_vma=False,
    )
```

```python
import functools

import jax
import jax.numpy as jnp
from jax import lax
from jax.experimental import pallas as pl
from jax.experimental.pallas import tpu as pltpu
from jax.sharding import PartitionSpec as P

KEY_HEADS = 8
HEAD_WIDTH = 64
FF = 1024
QUERY_PER_KEY = 3
QUERY_CHANNELS = 1536
KEY_CHANNELS = 512

norm_epsilon = 1e-05
beta_first = 0.9
beta_second = 0.99
adam_epsilon = 1e-08
weight_decay = 0.01
learn_rate = 0.5
ratio_epsilon = 1e-06
score_masked = -1e30
highest_mode = lax.Precision.HIGHEST


BF = jnp.bfloat16
F32 = jnp.float32
AXES = ("ctx", "fsdp")


def rms_norm(values, gain_vec):
    scaling = lax.rsqrt(jnp.mean(values * values, axis=-1, keepdims=True) + norm_epsilon)
    return values * scaling * gain_vec


def routing(logits, chosen):
    probabilities = jax.nn.softmax(logits, axis=-1)
    picked = jnp.sum(jnp.where(chosen, probabilities[:, None, :], 0.0), axis=2)
    return picked / jnp.sum(picked, axis=1, keepdims=True)


def adam_ratio(weight, gradient, first_old, second_old, step_count):
    tensor = weight.astype(F32)
    bias_one = 1.0 - jnp.power(beta_first, step_count)
    bias_two = 1.0 - jnp.power(beta_second, step_count)
    first_new = beta_first * first_old + (1.0 - beta_first) * gradient
    second_new = beta_second * second_old + (1.0 - beta_second) * gradient * gradient
    step_ratio = (
        first_new / bias_one / (jnp.sqrt(second_new / bias_two) + adam_epsilon)
        + weight_decay * tensor
    )
    return (first_new, second_new, step_ratio)


def nt(left, right):
    return lax.dot_general(left, right, (((1,), (1,)), ((), ())), preferred_element_type=F32)


def tn(left, right):
    return lax.dot_general(left, right, (((0,), (0,)), ((), ())), preferred_element_type=F32)


def nn(left, right):
    return jnp.dot(left, right, preferred_element_type=F32)


def tie(value, *others):
    return lax.optimization_barrier((value, *others))[0]


def three_parts(value):
    high = lax.reduce_precision(value, 8, 7)
    rest = value - high
    middle = lax.reduce_precision(rest, 8, 7)
    parts = jnp.concatenate([high, middle, rest - middle], axis=1).astype(BF)
    return jnp.pad(parts, ((0, 0), (0, 125)))


def three(ref, head, rows):
    base = head * QUERY_PER_KEY * HEAD_WIDTH
    return jnp.concatenate(
        [
            ref[:, base + g * HEAD_WIDTH : base + (g + 1) * HEAD_WIDTH]
            for g in range(QUERY_PER_KEY)
        ],
        axis=0,
    )


def put_three(ref, head, rows, turned):
    base = head * QUERY_PER_KEY * HEAD_WIDTH
    for g in range(QUERY_PER_KEY):
        part = turned[:, g * rows : (g + 1) * rows]
        ref[:, base + g * HEAD_WIDTH : base + (g + 1) * HEAD_WIDTH] = part.T.astype(ref.dtype)


def fill_bias(low_ref, bias, rows, window):
    @pl.when(pl.program_id(0) == 0)
    def _():
        def step(block, _):
            start = pl.multiple_of(block * rows, rows)
            key_pos = start + lax.broadcasted_iota(jnp.int32, (rows, rows), 0)
            top = lax.broadcasted_iota(jnp.int32, (rows, rows), 1) + (window - rows)
            allowed = (key_pos >= low_ref[...]) & (key_pos <= top)
            bias[pl.ds(start, rows), :] = jnp.where(allowed, 0.0, score_masked)
            return 0

        lax.fori_loop(0, window // rows, step, 0)


def attend_kernel(first_ref, low_ref, q_ref, k_ref, v_ref, o_ref, turned_ref, lse_ref, bias):
    rows, window = q_ref.shape[0], k_ref.shape[0]
    wide = QUERY_PER_KEY * rows
    fill_bias(low_ref, bias, rows, window)
    first = first_ref[0]
    for head in range(2):
        queries = three(q_ref, head, rows) * jnp.asarray(0.125, BF)
        lanes = slice(head * HEAD_WIDTH, (head + 1) * HEAD_WIDTH)

        def step(block, state):
            top, total, out = state
            span = pl.ds(pl.multiple_of(block * rows, rows), rows)
            shift = bias[span, :]
            scores = nt(k_ref[span, lanes], queries) + jnp.concatenate([shift] * QUERY_PER_KEY, 1)
            top_new = jnp.maximum(top, jnp.max(scores, axis=0, keepdims=True))
            weights = jnp.exp(scores - top_new)
            shrink = jnp.exp(top - top_new)
            total = total * shrink + jnp.sum(weights, axis=0, keepdims=True)
            out = out * shrink + tn(v_ref[span, lanes], weights.astype(BF))
            return (top_new, total, out)

        top, total, out = lax.fori_loop(
            first,
            window // rows,
            step,
            (
                jnp.full((1, wide), score_masked, F32),
                jnp.zeros((1, wide), F32),
                jnp.zeros((HEAD_WIDTH, wide), F32),
            ),
        )
        out = out / total
        turned_ref[head] = out
        lse_ref[head] = top + jnp.log(total)
        put_three(o_ref, head, rows, out)


def attend_grad_kernel(
    first_ref, low_ref, q_ref, k_ref, v_ref, do_ref, turned_ref, lse_ref, dq_ref, dk_ref, dv_ref, bias
):
    rows, window = q_ref.shape[0], k_ref.shape[0]
    wide = QUERY_PER_KEY * rows
    fill_bias(low_ref, bias, rows, window)
    first = first_ref[0]
    dk_ref[...] = jnp.zeros_like(dk_ref)
    dv_ref[...] = jnp.zeros_like(dv_ref)
    for head in range(2):
        queries = three(q_ref, head, rows) * jnp.asarray(0.125, BF)
        grads = three(do_ref, head, rows)
        delta = jnp.sum(grads.astype(F32).T * turned_ref[head], axis=0, keepdims=True)
        norm = lse_ref[head]
        lanes = slice(head * HEAD_WIDTH, (head + 1) * HEAD_WIDTH)

        def step(block, total):
            span = pl.ds(pl.multiple_of(block * rows, rows), rows)
            shift = bias[span, :]
            keys = k_ref[span, lanes]
            scores = nt(keys, queries) + jnp.concatenate([shift] * QUERY_PER_KEY, 1)
            weights = jnp.exp(scores - norm)
            prob_grad = nt(v_ref[span, lanes], grads)
            score_grad = (weights * (prob_grad - delta)).astype(BF)
            dv_ref[span, lanes] = nn(weights.astype(BF), grads).astype(BF)
            dk_ref[span, lanes] = nn(score_grad, queries).astype(BF)
            return total + tn(keys, score_grad)

        total = lax.fori_loop(first, window // rows, step, jnp.zeros((HEAD_WIDTH, wide), F32))
        put_three(dq_ref, head, rows, total * 0.125)


def attention_specs(rows, window):
    pair = 2 * QUERY_PER_KEY * HEAD_WIDTH
    pairs = KEY_HEADS // 2
    q_spec = pl.BlockSpec((rows, pair), lambda p: (0, p))
    k_spec = pl.BlockSpec((window, 2 * HEAD_WIDTH), lambda p: (0, p))
    v_spec = pl.BlockSpec((window, 2 * HEAD_WIDTH), lambda p: (0, p + pairs))
    turned = pl.BlockSpec((2, HEAD_WIDTH, QUERY_PER_KEY * rows), lambda p: (p, 0, 0))
    lse = pl.BlockSpec((2, 1, QUERY_PER_KEY * rows), lambda p: (p, 0, 0))
    first = pl.BlockSpec(memory_space=pltpu.SMEM)
    low = pl.BlockSpec((1, rows), lambda p: (0, 0))
    return pairs, q_spec, k_spec, v_spec, turned, lse, first, low


def attend(first, low, queries, keys_values):
    rows, window = queries.shape[0], keys_values.shape[0]
    pairs, q_spec, k_spec, v_spec, turned, lse, first_spec, low_spec = attention_specs(rows, window)
    wide = QUERY_PER_KEY * rows
    work = KEY_HEADS * wide * window
    return pl.pallas_call(
        attend_kernel,
        grid=(pairs,),
        in_specs=[first_spec, low_spec, q_spec, k_spec, v_spec],
        out_specs=[q_spec, turned, lse],
        out_shape=[
            jax.ShapeDtypeStruct((rows, QUERY_CHANNELS), BF),
            jax.ShapeDtypeStruct((KEY_HEADS, HEAD_WIDTH, wide), F32),
            jax.ShapeDtypeStruct((KEY_HEADS, 1, wide), F32),
        ],
        scratch_shapes=[pltpu.VMEM((window, rows), F32)],
        compiler_params=pltpu.CompilerParams(vmem_limit_bytes=40 << 20),
        cost_estimate=pl.CostEstimate(
            flops=4 * work * HEAD_WIDTH, transcendentals=work, bytes_accessed=8 << 20
        ),
        name="attend",
    )(first, low, queries, keys_values, keys_values)


def attend_grad(first, low, queries, keys_values, out_grad, turned_out, lse_rows):
    rows, window = queries.shape[0], keys_values.shape[0]
    pairs, q_spec, k_spec, v_spec, turned, lse, first_spec, low_spec = attention_specs(rows, window)
    wide = QUERY_PER_KEY * rows
    work = KEY_HEADS * wide * window
    return pl.pallas_call(
        attend_grad_kernel,
        grid=(pairs,),
        in_specs=[first_spec, low_spec, q_spec, k_spec, v_spec, q_spec, turned, lse],
        out_specs=[q_spec, k_spec, k_spec],
        out_shape=[
            jax.ShapeDtypeStruct((rows, QUERY_CHANNELS), BF),
            jax.ShapeDtypeStruct((window, KEY_CHANNELS), BF),
            jax.ShapeDtypeStruct((window, KEY_CHANNELS), BF),
        ],
        scratch_shapes=[pltpu.VMEM((window, rows), F32)],
        compiler_params=pltpu.CompilerParams(vmem_limit_bytes=40 << 20),
        cost_estimate=pl.CostEstimate(
            flops=10 * work * HEAD_WIDTH, transcendentals=work, bytes_accessed=12 << 20
        ),
        name="attend_grad",
    )(first, low, queries, keys_values, keys_values, out_grad, turned_out, lse_rows)


class Grid:
    def __init__(self, ctx, fsdp):
        self.ctx, self.fsdp = ctx, fsdp
        self.count = ctx * fsdp
        self.his = ctx // 2
        self.me = lax.axis_index("ctx") * fsdp + lax.axis_index("fsdp")
        self.lo = lax.rem(lax.axis_index("ctx"), 2)
        self.hi = lax.div(lax.axis_index("ctx"), 2)
        self.lo_mask = fsdp
        self.x_masks = []
        mask = fsdp // 2
        while mask > 1:
            self.x_masks.append(mask)
            mask //= 2

    def swap(self, value, mask):
        return lax.ppermute(value, AXES, [(i, i ^ mask) for i in range(self.count)])

    def shift_hi(self, value, by):
        step = by * 2 * self.fsdp
        pairs = [(i, i + step) for i in range(self.count) if 0 <= i + step < self.count]
        return lax.ppermute(value, AXES, pairs)

    def bit(self, mask):
        return lax.rem(lax.div(self.me, mask), 2)

    def ordered(self, own, got, mask):
        second = self.bit(mask) == 1
        return (jnp.where(second, got, own), jnp.where(second, own, got))

    def gather_hi(self, value):
        return [self.swap(value, m * 2 * self.fsdp) for m in range(1, self.his)]

    def order_hi(self, own, got):
        parts = [own] + got
        span = 1
        while span < self.his:
            odd = lax.rem(lax.div(self.hi, span), 2) == 1
            parts = [jnp.where(odd, parts[j ^ span], parts[j]) for j in range(self.his)]
            span *= 2
        return jnp.stack(parts, axis=0)

    def join(self, value, mask, axis, last=None):
        got = self.swap(value, mask)
        if last is not None:
            got = tie(got, last)
        return jnp.stack(self.ordered(value, got, mask), axis=axis)

    def gather_one(self, held, split):
        left, right = held[:, :, :split], held[:, :, split:]
        left = self.join(left, self.lo_mask, 1)
        for place, mask in enumerate(self.x_masks):
            right = self.join(right, mask, place + 1)
        return left, right

    def gather_two(self, left, right, last=None):
        for place, mask in enumerate(self.x_masks):
            left = self.join(left, mask, place + 2, last)
        return left, self.join(right, self.lo_mask, 1, last)

    def gather_core(self, value):
        value = jnp.stack(self.ordered(value, self.swap(value, 1), 1), axis=value.ndim - 2)
        return value.reshape(-1, value.shape[-1])

    def halve(self, value, axis, mask):
        mine = self.bit(mask)
        keep = lax.dynamic_index_in_dim(value, mine, axis, keepdims=False)
        send = lax.dynamic_index_in_dim(value, 1 - mine, axis, keepdims=False)
        got = self.swap(send.astype(BF), mask)
        return keep.astype(F32) + got.astype(F32)

    def scatter_core(self, value):
        bits = len(self.x_masks)
        rows = value.shape[0] // self.count
        value = value.reshape((self.his, 2) + (2,) * bits + (2, rows, value.shape[1]))
        return self.halve(value, 2 + bits, 1)

    def scatter_lo(self, value):
        return self.halve(value, 1, self.lo_mask)

    def scatter_x(self, value, after_lo):
        for mask in self.x_masks:
            value = self.halve(value, 1 if after_lo else 2, mask)
        return value

    def scatter_hi(self, value):
        total = lax.dynamic_index_in_dim(value, self.hi, 0, keepdims=False).astype(F32)
        for m in range(1, self.his):
            other = jnp.bitwise_xor(self.hi, m)
            send = lax.dynamic_index_in_dim(value, other, 0, keepdims=False).astype(BF)
            total = total + self.swap(send, m * 2 * self.fsdp).astype(F32)
        return total

    def everyone(self, value):
        mask = 1
        while mask < self.count:
            value = value + self.swap(value, mask)
            mask *= 2
        return value


def per_device(
    ctx,
    fsdp,
    tokens,
    segment_ids,
    routes,
    upstream,
    step,
    qkv_weight,
    qkv_first,
    qkv_second,
    proj_weight,
    proj_first,
    proj_second,
    router_weight,
    router_first,
    router_second,
    norm_gains,
    gains_first,
    gains_second,
    gate_up,
    gate_up_first,
    gate_up_second,
    down_weight,
    down_first,
    down_second,
):
    grid = Grid(ctx, fsdp)
    rows = tokens.shape[1]
    width = tokens.shape[2]
    seq_len = segment_ids.shape[1]
    experts = router_weight.shape[1]
    capacity = 3 * rows // experts
    hops = (seq_len // 2) // (2 * rows)
    window = (2 * hops + 1) * rows
    groups = [[2 * h + l for h in range(grid.his)] for l in range(2)]
    owned = (qkv_weight, proj_weight, router_weight, norm_gains, gate_up, down_weight)
    step_counts = step.astype(F32)
    lo = grid.lo

    def mine(shards):
        return lax.dynamic_index_in_dim(shards, lo, 0, keepdims=False)

    def others(shards):
        return lax.dynamic_index_in_dim(shards, 1 - lo, 0, keepdims=False)

    def cross(value):
        return grid.swap(value, grid.lo_mask)

    def both_rows(keep, got):
        return jnp.concatenate(grid.ordered(keep, got, grid.lo_mask), axis=0)

    def gather_experts(pair):
        return lax.all_gather(pair, "ctx", axis=0, tiled=True, axis_index_groups=groups)

    small = jnp.concatenate(
        [
            router_weight,
            norm_gains,
            jnp.zeros((router_weight.shape[0], 128 - experts - 2), BF),
        ],
        axis=1,
    )
    split = QUERY_CHANNELS
    half = QUERY_CHANNELS // 2
    qkv_own = jnp.concatenate([qkv_weight, small], axis=1)
    qkv_got = grid.gather_hi(qkv_own)
    own = tokens[0]
    chain = [own, grid.shift_hi(tie(own, qkv_got[0], qkv_got[-1]), 1)]
    gate_up_got = cross(others(gate_up))

    qkv_left, qkv_right = grid.gather_one(grid.order_hi(qkv_own, qkv_got), split)
    for _ in range(1, hops):
        chain.append(grid.shift_hi(tie(chain[-1], qkv_left, qkv_right), 1))
    across = [cross(jnp.where(lo == 0, chain[k - 1], chain[k])) for k in range(1, hops + 1)]
    proj_got = grid.gather_hi(tie(proj_weight, qkv_got[0], qkv_got[-1]))

    gate_up_pair = both_rows(mine(gate_up), gate_up_got)
    full_gate_up = gather_experts(tie(gate_up_pair, chain[1], qkv_left, qkv_right, *proj_got))
    down_got = cross(tie(others(down_weight), across[hops - 1]))
    full_down = gather_experts(both_rows(mine(down_weight), down_got))

    qkv_left, qkv_right = grid.gather_two(qkv_left, qkv_right)
    upstream_held = tie(upstream[0], qkv_left, qkv_right)
    proj_held = tie(grid.order_hi(proj_weight, proj_got), qkv_left, qkv_right)
    proj_left, proj_right = grid.gather_one(proj_held, half)

    numbers = jnp.arange(experts, dtype=jnp.int32)
    chosen = routes[0][:, :, None] == numbers[None, None, :]
    partners = 2 * fsdp
    flat_routes = routes[0].reshape(-1)
    onehot = (flat_routes[:, None] == numbers[None, :]).astype(jnp.int32)
    earlier = jnp.cumsum(onehot, axis=0) - onehot
    slot_rank = jnp.sum(earlier * onehot, axis=1)
    home = lax.rem(flat_routes, 2) * fsdp + lax.div(flat_routes, 2)
    relative = jnp.bitwise_xor(home, lax.rem(grid.me, partners))
    positions = (relative * capacity + slot_rank).reshape(rows, 2)
    slots = experts * capacity
    slot_ids = jnp.arange(slots, dtype=jnp.int32)
    put = [(slot_ids[:, None] == positions[None, :, k]).astype(BF) for k in range(2)]
    put_both = put[0] + put[1]
    put_wide = jnp.concatenate(put, axis=1)

    def exchange(sent):
        sent = sent.reshape(partners, capacity, sent.shape[1])
        return [sent[0]] + [grid.swap(sent[m], m) for m in range(1, partners)]

    def rows_of(pieces):
        return jnp.concatenate([piece[:, :width] for piece in pieces], axis=0)

    def sides_of(pieces):
        return jnp.concatenate([piece[:, width:] for piece in pieces], axis=0)

    dy_pieces = exchange(nn(put_both, upstream_held).astype(BF))
    qkv_left = grid.gather_core(qkv_left)
    qkv_right = grid.gather_core(qkv_right)
    full_small = qkv_right[:, 2 * KEY_CHANNELS :]
    qkv_right = qkv_right[:, : 2 * KEY_CHANNELS]
    full_router = full_small[:, :experts]
    full_gains = full_small[:, experts : experts + 2].astype(F32)
    attn_gain, moe_gain = full_gains[:, 0], full_gains[:, 1]

    blocks = [own]
    for k in range(1, hops + 1):
        blocks = [chain[k], across[k - 1]] + blocks
    token_f = own.astype(F32)
    normed, norm_back = jax.vjp(rms_norm, token_f, attn_gain)
    hidden = normed.astype(BF)
    seen = jnp.concatenate(blocks[:-1], axis=0)
    earlier_hidden = rms_norm(seen.astype(F32), attn_gain).astype(BF)
    hidden_window = jnp.concatenate([earlier_hidden, hidden], axis=0)
    queries = nn(hidden, qkv_left).astype(BF)
    keys_values = nn(hidden_window, qkv_right).astype(BF)
    proj_left, proj_right = grid.gather_two(proj_left, proj_right, keys_values)
    proj_left = grid.gather_core(proj_left)
    proj_right = grid.gather_core(proj_right)

    segments = segment_ids[0]
    start_own = lax.axis_index("ctx") * rows
    query_seg = lax.dynamic_slice_in_dim(segments, start_own, rows, 0)
    doc_start = jnp.sum((segments[None, :] < query_seg[:, None]).astype(jnp.int32), axis=1)
    low = (doc_start - start_own + (window - rows))[None, :]
    first = lax.div(jnp.maximum(low[0, :1], 0), rows)
    attended, turned_out, lse_rows = attend(first, low, queries, keys_values)

    branch = nt(attended[:, :half], proj_left) + nt(attended[:, half:], proj_right)
    middle = token_f + branch
    second_norm, second_back = jax.vjp(rms_norm, middle, moe_gain)
    second = second_norm.astype(BF)
    logits = nn(second, full_router)
    combine, routing_back = jax.vjp(lambda values: routing(values, chosen), logits)
    wide_rows = jnp.concatenate(
        [
            jnp.concatenate([second, three_parts(combine[:, k : k + 1])], axis=1)
            for k in range(2)
        ],
        axis=0,
    )
    sent_rows = nn(put_wide, wide_rows).astype(BF)
    dy_rows = jnp.concatenate([tie(piece, sent_rows) for piece in dy_pieces], axis=0)
    arrived_pieces = exchange(sent_rows)
    arrived = rows_of(arrived_pieces)
    shares = jnp.sum(sides_of(arrived_pieces).astype(F32), axis=1, keepdims=True)
    back_arrived = (shares * dy_rows.astype(F32)).astype(BF)

    both_parts = nn(arrived, full_gate_up)
    gates = both_parts[:, :FF]
    ups = both_parts[:, FF:]
    sigmoid_gate = jax.nn.sigmoid(gates)
    silu_gate = gates * sigmoid_gate
    activated = lax.optimization_barrier((silu_gate * ups).astype(BF))

    def reduce_experts(full):
        return lax.psum_scatter(
            full, "ctx", scatter_dimension=0, tiled=True, axis_index_groups=groups
        )

    def own_rows(part):
        part = part.reshape(2, part.shape[0] // 2, part.shape[1])
        both = grid.ordered(mine(part), cross(others(part)), grid.lo_mask)
        return jnp.stack(both, axis=0).astype(F32)

    down_full = tn(activated, back_arrived).astype(BF)
    down_part = reduce_experts(down_full)
    full_down = tie(full_down, down_full)
    act_grad = nt(back_arrived, full_down)
    gate_grad = act_grad * ups * (sigmoid_gate + silu_gate * (1.0 - sigmoid_gate))
    up_grad = act_grad * silu_gate
    both_grad = jnp.concatenate([gate_grad, up_grad], axis=-1).astype(BF)
    produced = nn(activated, full_down).astype(BF)
    share_grads = jnp.sum(produced.astype(F32) * dy_rows.astype(F32), axis=1, keepdims=True)
    row_grads = jnp.concatenate(
        [nt(both_grad, full_gate_up).astype(BF), three_parts(share_grads)], axis=1
    )
    back_pieces = exchange(row_grads)
    gate_up_full = tn(arrived, tie(both_grad, back_pieces[1])).astype(BF)
    gate_up_part = reduce_experts(gate_up_full)
    back_pieces = [tie(piece, gate_up_full) for piece in back_pieces]
    back_returned = rows_of(back_pieces)
    back_sides = sides_of(back_pieces)

    grad_out = upstream[0].astype(F32)
    combine_grad = jnp.stack(
        [jnp.sum(tn(put[k], back_sides), axis=1) for k in range(2)], axis=1
    )
    copy_grads = tn(put_both, back_returned)
    (logit_grad,) = routing_back(combine_grad)
    router_f = full_router.astype(F32)
    second_grad = copy_grads + jnp.dot(
        logit_grad, router_f.T, precision=highest_mode, preferred_element_type=F32
    )
    router_full = jnp.dot(
        second.astype(F32).T, logit_grad, precision=highest_mode, preferred_element_type=F32
    )
    middle_norm_grad, moe_gain_grad = second_back(second_grad)
    middle_grad = grad_out + middle_norm_grad
    middle_low = middle_grad.astype(BF)
    out_grad = jnp.concatenate(
        [nn(middle_low, proj_left).astype(BF), nn(middle_low, proj_right).astype(BF)], axis=1
    )
    proj_cut = KEY_CHANNELS
    proj_one = tn(middle_low, attended[:, :proj_cut]).astype(BF)
    proj_two = tn(middle_low, attended[:, proj_cut:]).astype(BF)
    side = jnp.concatenate(
        [
            router_full.astype(BF),
            moe_gain_grad[:, None].astype(BF),
            jnp.zeros((width, 128 - experts - 1), BF),
        ],
        axis=1,
    )
    out_grad = tie(out_grad, proj_one, proj_two)
    proj_one = grid.scatter_core(proj_one)
    proj_two = grid.scatter_core(jnp.concatenate([proj_two, side], axis=1))

    query_grad, key_part, value_part = attend_grad(
        first, low, queries, keys_values, out_grad, turned_out, lse_rows
    )
    kv_part = jnp.concatenate([key_part, value_part], axis=1)
    parts = [kv_part[j * rows : (j + 1) * rows] for j in range(2 * hops + 1)]
    crossed = jnp.concatenate([parts[2 * (hops - k) + 1] for k in range(1, hops + 1)], axis=0)
    kept = [parts[2 * hops]] + [parts[2 * (hops - k)] for k in range(1, hops + 1)]
    crossed = cross(crossed)
    got = [None] + [crossed[k * rows : (k + 1) * rows] for k in range(hops)]

    qkv_two = grid.scatter_core(tn(hidden_window, kv_part).astype(BF))
    qkv_one = grid.scatter_core(tn(hidden, query_grad).astype(BF))
    left = jnp.concatenate([qkv_one.astype(BF), proj_one.astype(BF)], axis=-1)
    right = jnp.concatenate([qkv_two.astype(BF), proj_two.astype(BF)], axis=-1)
    left_one = grid.scatter_x(left, False)
    right_one = grid.scatter_lo(right)
    sums = []
    for k in range(hops + 1):
        after = got[k + 1].astype(F32) if k < hops else 0.0
        here = got[k].astype(F32) if k > 0 else 0.0
        sums.append(kept[k].astype(F32) + jnp.where(lo == 1, here, after))
    left_two = grid.scatter_lo(left_one)
    right_two = grid.scatter_x(right_one, True)
    running = tie(sums[hops].astype(BF), left, right)
    for k in range(hops, 0, -1):
        moved = tie(grid.shift_hi(running, -1), left_one, right_one)
        running = (sums[k - 1] + moved.astype(F32)).astype(BF)
    kv_grad = tie(running, left_two, right_two)
    down_grad = own_rows(down_part)
    gate_up_grad = own_rows(tie(gate_up_part, down_grad))
    total = grid.scatter_hi(jnp.concatenate([left_two, right_two], axis=-1))
    total = tie(total, gate_up_grad)
    places = [0, QUERY_CHANNELS, QUERY_CHANNELS + proj_cut]
    places += [places[2] + 2 * KEY_CHANNELS, places[2] + 2 * KEY_CHANNELS + QUERY_CHANNELS - proj_cut]
    qkv_grad = jnp.concatenate([total[:, : places[1]], total[:, places[2] : places[3]]], axis=1)
    proj_grad = jnp.concatenate(
        [total[:, places[1] : places[2]], total[:, places[3] : places[4]]], axis=1
    )
    router_grad = total[:, places[4] : places[4] + experts]
    moe_own = total[:, places[4] + experts]

    query_after = tie(query_grad, left, right)
    hidden_grad = (
        nt(query_after, qkv_left) + nt(kv_grad, qkv_right)
    )
    token_norm_grad, attn_gain_grad = norm_back(hidden_grad)
    token_grad = (middle_grad + token_norm_grad)[None]
    attn_sum = grid.everyone(attn_gain_grad.reshape(-1, 128))
    attn_own = lax.dynamic_index_in_dim(attn_sum.reshape(grid.count, -1), grid.me, 0, keepdims=False)
    gains_grad = jnp.stack([attn_own, moe_own], axis=1)

    returned = jnp.concatenate(exchange(tie(produced, left_two, right_two)), axis=0)
    picked = [tn(put[k], returned) for k in range(2)]
    result = middle + combine[:, :1] * picked[0] + combine[:, 1:] * picked[1]
    block_out = result.astype(BF)[None]

    gradients = (qkv_grad, proj_grad, router_grad, gains_grad, gate_up_grad, down_grad)
    firsts = (qkv_first, proj_first, router_first, gains_first, gate_up_first, down_first)
    seconds = (qkv_second, proj_second, router_second, gains_second, gate_up_second, down_second)
    states = [
        adam_ratio(
            owned[number], gradients[number], firsts[number], seconds[number], step_counts[number]
        )
        for number in range(6)
    ]
    squares = [jnp.sum(jnp.square(tensor.astype(F32))) for tensor in owned]
    squares += [jnp.sum(entry[2] * entry[2]) for entry in states]
    lane = lax.broadcasted_iota(jnp.int32, (1, 128), 1)
    own_sums = sum(jnp.where(lane == k, square, 0.0) for k, square in enumerate(squares))
    sums_all = grid.everyone(own_sums)
    weight_tot, ratio_tot = sums_all[0, :6], sums_all[0, 6:12]
    trust_ratio = jnp.sqrt(weight_tot) * lax.rsqrt(ratio_tot + ratio_epsilon)
    new_weights = [
        owned[number].astype(F32) - learn_rate * trust_ratio[number] * states[number][2]
        for number in range(6)
    ]
    matrix_norms = 0.5 * jnp.log(jnp.stack([weight_tot, ratio_tot + ratio_epsilon]))
    return (
        block_out,
        token_grad,
        *gradients,
        *[entry[0] for entry in states],
        *[entry[1] for entry in states],
        *new_weights,
        matrix_norms,
    )


def solution(mesh):
    rows = P(("ctx", "fsdp"), None)
    tokens = P("fsdp", "ctx", None)
    weights = [rows] * 4 + [tokens] * 2
    return jax.shard_map(
        functools.partial(per_device, mesh.shape["ctx"], mesh.shape["fsdp"]),
        mesh=mesh,
        in_specs=(tokens, P("fsdp", None), tokens, tokens, P())
        + tuple(spec for spec in weights for _ in range(3)),
        out_specs=(tokens, tokens) + tuple(weights) * 4 + (P(),),
        check_vma=False,
    )
```

```python
import functools

import jax
import jax.numpy as jnp
from jax import lax
from jax.experimental import pallas as pl
from jax.experimental.pallas import tpu as pltpu
from jax.sharding import PartitionSpec as P

KEY_HEADS = 8
HEAD_WIDTH = 64
FF = 1024
QUERY_PER_KEY = 3
QUERY_CHANNELS = 1536
KEY_CHANNELS = 512

norm_epsilon = 1e-05
beta_first = 0.9
beta_second = 0.99
adam_epsilon = 1e-08
weight_decay = 0.01
learn_rate = 0.5
ratio_epsilon = 1e-06
score_masked = -1e30
highest_mode = lax.Precision.HIGHEST


BF = jnp.bfloat16
F32 = jnp.float32
AXES = ("ctx", "fsdp")


def rms_norm(values, gain_vec):
    scaling = lax.rsqrt(jnp.mean(values * values, axis=-1, keepdims=True) + norm_epsilon)
    return values * scaling * gain_vec


def routing(logits, chosen):
    probabilities = jax.nn.softmax(logits, axis=-1)
    picked = jnp.sum(jnp.where(chosen, probabilities[:, None, :], 0.0), axis=2)
    return picked / jnp.sum(picked, axis=1, keepdims=True)


def adam_ratio(weight, gradient, first_old, second_old, step_count):
    tensor = weight.astype(F32)
    bias_one = 1.0 - jnp.power(beta_first, step_count)
    bias_two = 1.0 - jnp.power(beta_second, step_count)
    first_new = beta_first * first_old + (1.0 - beta_first) * gradient
    second_new = beta_second * second_old + (1.0 - beta_second) * gradient * gradient
    step_ratio = (
        first_new / bias_one / (jnp.sqrt(second_new / bias_two) + adam_epsilon)
        + weight_decay * tensor
    )
    return (first_new, second_new, step_ratio)


def nt(left, right):
    return lax.dot_general(left, right, (((1,), (1,)), ((), ())), preferred_element_type=F32)


def tn(left, right):
    return lax.dot_general(left, right, (((0,), (0,)), ((), ())), preferred_element_type=F32)


def nn(left, right):
    return jnp.dot(left, right, preferred_element_type=F32)


def tie(value, *others):
    return lax.optimization_barrier((value, *others))[0]


def three_parts(value):
    high = lax.reduce_precision(value, 8, 7)
    rest = value - high
    middle = lax.reduce_precision(rest, 8, 7)
    parts = jnp.concatenate([high, middle, rest - middle], axis=1).astype(BF)
    return jnp.pad(parts, ((0, 0), (0, 125)))


def three(ref, head, rows):
    base = head * QUERY_PER_KEY * HEAD_WIDTH
    return jnp.concatenate(
        [
            ref[:, base + g * HEAD_WIDTH : base + (g + 1) * HEAD_WIDTH]
            for g in range(QUERY_PER_KEY)
        ],
        axis=0,
    )


def put_three(ref, head, rows, turned):
    base = head * QUERY_PER_KEY * HEAD_WIDTH
    for g in range(QUERY_PER_KEY):
        part = turned[:, g * rows : (g + 1) * rows]
        ref[:, base + g * HEAD_WIDTH : base + (g + 1) * HEAD_WIDTH] = part.T.astype(ref.dtype)


def fill_bias(low_ref, bias, rows, window):
    @pl.when(pl.program_id(0) == 0)
    def _():
        def step(block, _):
            start = pl.multiple_of(block * rows, rows)
            key_pos = start + lax.broadcasted_iota(jnp.int32, (rows, rows), 0)
            top = lax.broadcasted_iota(jnp.int32, (rows, rows), 1) + (window - rows)
            allowed = (key_pos >= low_ref[...]) & (key_pos <= top)
            bias[pl.ds(start, rows), :] = jnp.where(allowed, 0.0, score_masked)
            return 0

        lax.fori_loop(0, window // rows, step, 0)


def attend_kernel(first_ref, low_ref, q_ref, k_ref, v_ref, o_ref, turned_ref, lse_ref, bias):
    rows, window = q_ref.shape[0], k_ref.shape[0]
    wide = QUERY_PER_KEY * rows
    fill_bias(low_ref, bias, rows, window)
    first = first_ref[0]
    for head in range(2):
        queries = three(q_ref, head, rows) * jnp.asarray(0.125, BF)
        lanes = slice(head * HEAD_WIDTH, (head + 1) * HEAD_WIDTH)

        def step(block, state):
            top, total, out = state
            span = pl.ds(pl.multiple_of(block * rows, rows), rows)
            shift = bias[span, :]
            scores = nt(k_ref[span, lanes], queries) + jnp.concatenate([shift] * QUERY_PER_KEY, 1)
            top_new = jnp.maximum(top, jnp.max(scores, axis=0, keepdims=True))
            weights = jnp.exp(scores - top_new)
            shrink = jnp.exp(top - top_new)
            total = total * shrink + jnp.sum(weights, axis=0, keepdims=True)
            out = out * shrink + tn(v_ref[span, lanes], weights.astype(BF))
            return (top_new, total, out)

        top, total, out = lax.fori_loop(
            first,
            window // rows,
            step,
            (
                jnp.full((1, wide), score_masked, F32),
                jnp.zeros((1, wide), F32),
                jnp.zeros((HEAD_WIDTH, wide), F32),
            ),
        )
        out = out / total
        turned_ref[head] = out
        lse_ref[head] = top + jnp.log(total)
        put_three(o_ref, head, rows, out)


def attend_grad_kernel(
    first_ref, low_ref, q_ref, k_ref, v_ref, do_ref, turned_ref, lse_ref, dq_ref, dk_ref, dv_ref, bias
):
    rows, window = q_ref.shape[0], k_ref.shape[0]
    wide = QUERY_PER_KEY * rows
    fill_bias(low_ref, bias, rows, window)
    first = first_ref[0]
    dk_ref[...] = jnp.zeros_like(dk_ref)
    dv_ref[...] = jnp.zeros_like(dv_ref)
    for head in range(2):
        queries = three(q_ref, head, rows) * jnp.asarray(0.125, BF)
        grads = three(do_ref, head, rows)
        delta = jnp.sum(grads.astype(F32).T * turned_ref[head], axis=0, keepdims=True)
        norm = lse_ref[head]
        lanes = slice(head * HEAD_WIDTH, (head + 1) * HEAD_WIDTH)

        def step(block, total):
            span = pl.ds(pl.multiple_of(block * rows, rows), rows)
            shift = bias[span, :]
            keys = k_ref[span, lanes]
            scores = nt(keys, queries) + jnp.concatenate([shift] * QUERY_PER_KEY, 1)
            weights = jnp.exp(scores - norm)
            prob_grad = nt(v_ref[span, lanes], grads)
            score_grad = (weights * (prob_grad - delta)).astype(BF)
            dv_ref[span, lanes] = nn(weights.astype(BF), grads).astype(BF)
            dk_ref[span, lanes] = nn(score_grad, queries).astype(BF)
            return total + tn(keys, score_grad)

        total = lax.fori_loop(first, window // rows, step, jnp.zeros((HEAD_WIDTH, wide), F32))
        put_three(dq_ref, head, rows, total * 0.125)


def attention_specs(rows, window):
    pair = 2 * QUERY_PER_KEY * HEAD_WIDTH
    pairs = KEY_HEADS // 2
    q_spec = pl.BlockSpec((rows, pair), lambda p: (0, p))
    k_spec = pl.BlockSpec((window, 2 * HEAD_WIDTH), lambda p: (0, p))
    v_spec = pl.BlockSpec((window, 2 * HEAD_WIDTH), lambda p: (0, p + pairs))
    turned = pl.BlockSpec((2, HEAD_WIDTH, QUERY_PER_KEY * rows), lambda p: (p, 0, 0))
    lse = pl.BlockSpec((2, 1, QUERY_PER_KEY * rows), lambda p: (p, 0, 0))
    first = pl.BlockSpec(memory_space=pltpu.SMEM)
    low = pl.BlockSpec((1, rows), lambda p: (0, 0))
    return pairs, q_spec, k_spec, v_spec, turned, lse, first, low


def attend(first, low, queries, keys_values):
    rows, window = queries.shape[0], keys_values.shape[0]
    pairs, q_spec, k_spec, v_spec, turned, lse, first_spec, low_spec = attention_specs(rows, window)
    wide = QUERY_PER_KEY * rows
    work = KEY_HEADS * wide * window
    return pl.pallas_call(
        attend_kernel,
        grid=(pairs,),
        in_specs=[first_spec, low_spec, q_spec, k_spec, v_spec],
        out_specs=[q_spec, turned, lse],
        out_shape=[
            jax.ShapeDtypeStruct((rows, QUERY_CHANNELS), BF),
            jax.ShapeDtypeStruct((KEY_HEADS, HEAD_WIDTH, wide), F32),
            jax.ShapeDtypeStruct((KEY_HEADS, 1, wide), F32),
        ],
        scratch_shapes=[pltpu.VMEM((window, rows), F32)],
        compiler_params=pltpu.CompilerParams(vmem_limit_bytes=40 << 20),
        cost_estimate=pl.CostEstimate(
            flops=4 * work * HEAD_WIDTH, transcendentals=work, bytes_accessed=8 << 20
        ),
        name="attend",
    )(first, low, queries, keys_values, keys_values)


def attend_grad(first, low, queries, keys_values, out_grad, turned_out, lse_rows):
    rows, window = queries.shape[0], keys_values.shape[0]
    pairs, q_spec, k_spec, v_spec, turned, lse, first_spec, low_spec = attention_specs(rows, window)
    wide = QUERY_PER_KEY * rows
    work = KEY_HEADS * wide * window
    return pl.pallas_call(
        attend_grad_kernel,
        grid=(pairs,),
        in_specs=[first_spec, low_spec, q_spec, k_spec, v_spec, q_spec, turned, lse],
        out_specs=[q_spec, k_spec, k_spec],
        out_shape=[
            jax.ShapeDtypeStruct((rows, QUERY_CHANNELS), BF),
            jax.ShapeDtypeStruct((window, KEY_CHANNELS), BF),
            jax.ShapeDtypeStruct((window, KEY_CHANNELS), BF),
        ],
        scratch_shapes=[pltpu.VMEM((window, rows), F32)],
        compiler_params=pltpu.CompilerParams(vmem_limit_bytes=40 << 20),
        cost_estimate=pl.CostEstimate(
            flops=10 * work * HEAD_WIDTH, transcendentals=work, bytes_accessed=12 << 20
        ),
        name="attend_grad",
    )(first, low, queries, keys_values, keys_values, out_grad, turned_out, lse_rows)


class Grid:
    def __init__(self, ctx, fsdp):
        self.ctx, self.fsdp = ctx, fsdp
        self.count = ctx * fsdp
        self.his = ctx // 2
        self.me = lax.axis_index("ctx") * fsdp + lax.axis_index("fsdp")
        self.lo = lax.rem(lax.axis_index("ctx"), 2)
        self.hi = lax.div(lax.axis_index("ctx"), 2)
        self.lo_mask = fsdp
        self.x_masks = []
        mask = fsdp // 2
        while mask > 1:
            self.x_masks.append(mask)
            mask //= 2

    def swap(self, value, mask):
        return lax.ppermute(value, AXES, [(i, i ^ mask) for i in range(self.count)])

    def shift_hi(self, value, by):
        step = by * 2 * self.fsdp
        pairs = [(i, i + step) for i in range(self.count) if 0 <= i + step < self.count]
        return lax.ppermute(value, AXES, pairs)

    def bit(self, mask):
        return lax.rem(lax.div(self.me, mask), 2)

    def ordered(self, own, got, mask):
        second = self.bit(mask) == 1
        return (jnp.where(second, got, own), jnp.where(second, own, got))

    def gather_hi(self, value):
        return [self.swap(value, m * 2 * self.fsdp) for m in range(1, self.his)]

    def order_hi(self, own, got):
        parts = [own] + got
        span = 1
        while span < self.his:
            odd = lax.rem(lax.div(self.hi, span), 2) == 1
            parts = [jnp.where(odd, parts[j ^ span], parts[j]) for j in range(self.his)]
            span *= 2
        return jnp.stack(parts, axis=0)

    def join(self, value, mask, axis, last=None):
        got = self.swap(value, mask)
        if last is not None:
            got = tie(got, last)
        return jnp.stack(self.ordered(value, got, mask), axis=axis)

    def gather_one(self, held, split, last=None):
        left, right = held[:, :, :split], held[:, :, split:]
        left = self.join(left, self.lo_mask, 1, last)
        for place, mask in enumerate(self.x_masks):
            right = self.join(right, mask, place + 1, last)
        return left, right

    def gather_two(self, left, right, last=None):
        for place, mask in enumerate(self.x_masks):
            left = self.join(left, mask, place + 2, last)
        return left, self.join(right, self.lo_mask, 1, last)

    def gather_core(self, value):
        value = jnp.stack(self.ordered(value, self.swap(value, 1), 1), axis=value.ndim - 2)
        return value.reshape(-1, value.shape[-1])

    def halve(self, value, axis, mask):
        mine = self.bit(mask)
        keep = lax.dynamic_index_in_dim(value, mine, axis, keepdims=False)
        send = lax.dynamic_index_in_dim(value, 1 - mine, axis, keepdims=False)
        got = self.swap(send.astype(BF), mask)
        return keep.astype(F32) + got.astype(F32)

    def scatter_core(self, value):
        bits = len(self.x_masks)
        rows = value.shape[0] // self.count
        value = value.reshape((self.his, 2) + (2,) * bits + (2, rows, value.shape[1]))
        return self.halve(value, 2 + bits, 1)

    def scatter_lo(self, value):
        return self.halve(value, 1, self.lo_mask)

    def scatter_x(self, value, after_lo):
        for mask in self.x_masks:
            value = self.halve(value, 1 if after_lo else 2, mask)
        return value

    def scatter_hi(self, value):
        total = lax.dynamic_index_in_dim(value, self.hi, 0, keepdims=False).astype(F32)
        for m in range(1, self.his):
            other = jnp.bitwise_xor(self.hi, m)
            send = lax.dynamic_index_in_dim(value, other, 0, keepdims=False).astype(BF)
            total = total + self.swap(send, m * 2 * self.fsdp).astype(F32)
        return total

    def everyone(self, value):
        mask = 1
        while mask < self.count:
            value = value + self.swap(value, mask)
            mask *= 2
        return value


def per_device(
    ctx,
    fsdp,
    tokens,
    segment_ids,
    routes,
    upstream,
    step,
    qkv_weight,
    qkv_first,
    qkv_second,
    proj_weight,
    proj_first,
    proj_second,
    router_weight,
    router_first,
    router_second,
    norm_gains,
    gains_first,
    gains_second,
    gate_up,
    gate_up_first,
    gate_up_second,
    down_weight,
    down_first,
    down_second,
):
    grid = Grid(ctx, fsdp)
    rows = tokens.shape[1]
    width = tokens.shape[2]
    seq_len = segment_ids.shape[1]
    experts = router_weight.shape[1]
    capacity = 3 * rows // experts
    hops = (seq_len // 2) // (2 * rows)
    window = (2 * hops + 1) * rows
    groups = [[2 * h + l for h in range(grid.his)] for l in range(2)]
    owned = (qkv_weight, proj_weight, router_weight, norm_gains, gate_up, down_weight)
    step_counts = step.astype(F32)
    lo = grid.lo

    def mine(shards):
        return lax.dynamic_index_in_dim(shards, lo, 0, keepdims=False)

    def others(shards):
        return lax.dynamic_index_in_dim(shards, 1 - lo, 0, keepdims=False)

    def cross(value):
        return grid.swap(value, grid.lo_mask)

    def both_rows(keep, got):
        return jnp.concatenate(grid.ordered(keep, got, grid.lo_mask), axis=0)

    def gather_experts(pair):
        return lax.all_gather(pair, "ctx", axis=0, tiled=True, axis_index_groups=groups)

    small = jnp.concatenate(
        [
            router_weight,
            norm_gains,
            jnp.zeros((router_weight.shape[0], 128 - experts - 2), BF),
        ],
        axis=1,
    )
    split = QUERY_CHANNELS
    half = QUERY_CHANNELS // 2
    qkv_own = jnp.concatenate([qkv_weight, small], axis=1)
    qkv_got = grid.gather_hi(qkv_own)
    own = tokens[0]
    chain = [own, grid.shift_hi(tie(own, qkv_got[0], qkv_got[-1]), 1)]
    gate_up_got = cross(others(gate_up))

    qkv_left, qkv_right = grid.gather_one(grid.order_hi(qkv_own, qkv_got), split)
    for _ in range(1, hops):
        chain.append(grid.shift_hi(tie(chain[-1], qkv_left, qkv_right), 1))
    qkv_left, qkv_right = grid.gather_two(qkv_left, qkv_right)
    across = [cross(jnp.where(lo == 0, own, chain[1]))]
    for k in range(2, hops + 1):
        across.append(cross(tie(jnp.where(lo == 0, chain[k - 1], chain[k]), qkv_left, qkv_right)))
    proj_got = grid.gather_hi(tie(proj_weight, qkv_got[0], qkv_got[-1]))

    gate_up_pair = both_rows(mine(gate_up), gate_up_got)
    full_gate_up = gather_experts(tie(gate_up_pair, chain[hops], qkv_left, qkv_right, *proj_got))

    proj_held = tie(grid.order_hi(proj_weight, proj_got), qkv_left, qkv_right)

    numbers = jnp.arange(experts, dtype=jnp.int32)
    chosen = routes[0][:, :, None] == numbers[None, None, :]
    partners = 2 * fsdp
    flat_routes = routes[0].reshape(-1)
    onehot = (flat_routes[:, None] == numbers[None, :]).astype(jnp.int32)
    earlier = jnp.cumsum(onehot, axis=0) - onehot
    slot_rank = jnp.sum(earlier * onehot, axis=1)
    home = lax.rem(flat_routes, 2) * fsdp + lax.div(flat_routes, 2)
    relative = jnp.bitwise_xor(home, lax.rem(grid.me, partners))
    positions = (relative * capacity + slot_rank).reshape(rows, 2)
    slots = experts * capacity
    slot_ids = jnp.arange(slots, dtype=jnp.int32)
    put = [(slot_ids[:, None] == positions[None, :, k]).astype(BF) for k in range(2)]
    put_both = put[0] + put[1]
    put_wide = jnp.concatenate(put, axis=1)

    def exchange(sent):
        sent = sent.reshape(partners, capacity, sent.shape[1])
        return [sent[0]] + [grid.swap(sent[m], m) for m in range(1, partners)]

    def rows_of(pieces):
        return jnp.concatenate([piece[:, :width] for piece in pieces], axis=0)

    def sides_of(pieces):
        return jnp.concatenate([piece[:, width:] for piece in pieces], axis=0)

    qkv_left = grid.gather_core(qkv_left)
    qkv_right = grid.gather_core(qkv_right)
    full_small = qkv_right[:, 2 * KEY_CHANNELS :]
    qkv_right = qkv_right[:, : 2 * KEY_CHANNELS]
    full_router = full_small[:, :experts]
    full_gains = full_small[:, experts : experts + 2].astype(F32)
    attn_gain, moe_gain = full_gains[:, 0], full_gains[:, 1]

    blocks = [own]
    for k in range(1, hops + 1):
        blocks = [chain[k], across[k - 1]] + blocks
    token_f = own.astype(F32)
    normed, norm_back = jax.vjp(rms_norm, token_f, attn_gain)
    hidden = normed.astype(BF)
    seen = jnp.concatenate(blocks[:-1], axis=0)
    earlier_hidden = rms_norm(seen.astype(F32), attn_gain).astype(BF)
    hidden_window = jnp.concatenate([earlier_hidden, hidden], axis=0)
    queries = nn(hidden, qkv_left).astype(BF)
    keys_values = nn(hidden_window, qkv_right).astype(BF)
    proj_left, proj_right = grid.gather_one(proj_held, half, keys_values)
    proj_left, proj_right = grid.gather_two(proj_left, proj_right)
    down_got = cross(tie(others(down_weight), keys_values))
    full_down = gather_experts(both_rows(mine(down_weight), down_got))
    proj_left = grid.gather_core(proj_left)
    proj_right = grid.gather_core(proj_right)

    segments = segment_ids[0]
    start_own = lax.axis_index("ctx") * rows
    query_seg = lax.dynamic_slice_in_dim(segments, start_own, rows, 0)
    doc_start = jnp.sum((segments[None, :] < query_seg[:, None]).astype(jnp.int32), axis=1)
    low = (doc_start - start_own + (window - rows))[None, :]
    first = lax.div(jnp.maximum(low[0, :1], 0), rows)
    attended, turned_out, lse_rows = attend(first, low, queries, keys_values)

    branch = nt(attended[:, :half], proj_left) + nt(attended[:, half:], proj_right)
    middle = token_f + branch
    second_norm, second_back = jax.vjp(rms_norm, middle, moe_gain)
    second = second_norm.astype(BF)
    logits = nn(second, full_router)
    combine, routing_back = jax.vjp(lambda values: routing(values, chosen), logits)
    wide_rows = jnp.concatenate(
        [
            jnp.concatenate([second, three_parts(combine[:, k : k + 1])], axis=1)
            for k in range(2)
        ],
        axis=0,
    )
    sent_rows = nn(put_wide, wide_rows).astype(BF)
    arrived_pieces = exchange(sent_rows)
    dy_sent = tie(nn(put_both, tie(upstream[0], second)).astype(BF), arrived_pieces[1])
    dy_rows = jnp.concatenate(exchange(dy_sent), axis=0)
    arrived = rows_of(arrived_pieces)
    shares = jnp.sum(sides_of(arrived_pieces).astype(F32), axis=1, keepdims=True)
    back_arrived = (shares * dy_rows.astype(F32)).astype(BF)

    both_parts = nn(arrived, full_gate_up)
    gates = both_parts[:, :FF]
    ups = both_parts[:, FF:]
    sigmoid_gate = jax.nn.sigmoid(gates)
    silu_gate = gates * sigmoid_gate
    activated = lax.optimization_barrier((silu_gate * ups).astype(BF))

    def reduce_experts(full):
        return lax.psum_scatter(
            full, "ctx", scatter_dimension=0, tiled=True, axis_index_groups=groups
        )

    def own_rows(part):
        part = part.reshape(2, part.shape[0] // 2, part.shape[1])
        both = grid.ordered(mine(part), cross(others(part)), grid.lo_mask)
        return jnp.stack(both, axis=0).astype(F32)

    down_full = tn(activated, back_arrived).astype(BF)
    down_part = reduce_experts(down_full)
    full_down = tie(full_down, down_full)
    act_grad = nt(back_arrived, full_down)
    gate_grad = act_grad * ups * (sigmoid_gate + silu_gate * (1.0 - sigmoid_gate))
    up_grad = act_grad * silu_gate
    both_grad = jnp.concatenate([gate_grad, up_grad], axis=-1).astype(BF)
    produced = nn(activated, full_down).astype(BF)
    share_grads = jnp.sum(produced.astype(F32) * dy_rows.astype(F32), axis=1, keepdims=True)
    row_grads = jnp.concatenate(
        [nt(both_grad, full_gate_up).astype(BF), three_parts(share_grads)], axis=1
    )
    back_pieces = exchange(row_grads)
    gate_up_full = tn(arrived, tie(both_grad, back_pieces[1])).astype(BF)
    gate_up_part = reduce_experts(gate_up_full)
    back_pieces = [tie(piece, gate_up_full) for piece in back_pieces]
    back_returned = rows_of(back_pieces)
    back_sides = sides_of(back_pieces)

    grad_out = upstream[0].astype(F32)
    combine_grad = jnp.stack(
        [jnp.sum(tn(put[k], back_sides), axis=1) for k in range(2)], axis=1
    )
    copy_grads = tn(put_both, back_returned)
    (logit_grad,) = routing_back(combine_grad)
    router_f = full_router.astype(F32)
    second_grad = copy_grads + jnp.dot(
        logit_grad, router_f.T, precision=highest_mode, preferred_element_type=F32
    )
    router_full = jnp.dot(
        second.astype(F32).T,
        jnp.pad(logit_grad, ((0, 0), (0, 128 - experts))),
        precision=highest_mode,
        preferred_element_type=F32,
    )
    middle_norm_grad, moe_gain_grad = second_back(second_grad)
    middle_grad = grad_out + middle_norm_grad
    middle_low = middle_grad.astype(BF)
    out_grad = jnp.concatenate(
        [nn(middle_low, proj_left).astype(BF), nn(middle_low, proj_right).astype(BF)], axis=1
    )
    proj_cut = KEY_CHANNELS
    proj_one = tn(middle_low, attended[:, :proj_cut]).astype(BF)
    proj_two = tn(middle_low, attended[:, proj_cut:]).astype(BF)
    out_grad = tie(out_grad, proj_one, proj_two)
    proj_one = grid.scatter_core(proj_one)
    proj_two = grid.scatter_core(jnp.concatenate([proj_two, router_full.astype(BF)], axis=1))

    query_grad, key_part, value_part = attend_grad(
        first, low, queries, keys_values, out_grad, turned_out, lse_rows
    )
    kv_part = jnp.concatenate([key_part, value_part], axis=1)
    parts = [kv_part[j * rows : (j + 1) * rows] for j in range(2 * hops + 1)]
    crossed = jnp.concatenate([parts[2 * (hops - k) + 1] for k in range(1, hops + 1)], axis=0)
    kept = [parts[2 * hops]] + [parts[2 * (hops - k)] for k in range(1, hops + 1)]
    crossed = cross(crossed)
    got = [None] + [crossed[k * rows : (k + 1) * rows] for k in range(hops)]

    qkv_two = grid.scatter_core(tn(hidden_window, kv_part).astype(BF))
    qkv_one = grid.scatter_core(tn(hidden, query_grad).astype(BF))
    left = jnp.concatenate([qkv_one.astype(BF), proj_one.astype(BF)], axis=-1)
    right = jnp.concatenate([qkv_two.astype(BF), proj_two.astype(BF)], axis=-1)
    left_one = grid.scatter_x(left, False)
    right_one = grid.scatter_lo(right)
    sums = []
    for k in range(hops + 1):
        after = got[k + 1].astype(F32) if k < hops else 0.0
        here = got[k].astype(F32) if k > 0 else 0.0
        sums.append(kept[k].astype(F32) + jnp.where(lo == 1, here, after))
    left_two = grid.scatter_lo(left_one)
    right_two = grid.scatter_x(right_one, True)
    running = tie(sums[hops].astype(BF), left, right)
    for k in range(hops, 0, -1):
        moved = tie(grid.shift_hi(running, -1), left_one, right_one)
        running = (sums[k - 1] + moved.astype(F32)).astype(BF)
    merged = jnp.concatenate([left_two, right_two], axis=-1).astype(BF)
    merged = tie(merged, down_part, gate_up_part)
    kv_grad = tie(running, merged)
    down_grad = own_rows(down_part)
    gate_up_grad = own_rows(gate_up_part)
    total = grid.scatter_hi(merged)
    places = [0, QUERY_CHANNELS, QUERY_CHANNELS + proj_cut]
    places += [places[2] + 2 * KEY_CHANNELS, places[2] + 2 * KEY_CHANNELS + QUERY_CHANNELS - proj_cut]
    qkv_grad = jnp.concatenate([total[:, : places[1]], total[:, places[2] : places[3]]], axis=1)
    proj_grad = jnp.concatenate(
        [total[:, places[1] : places[2]], total[:, places[3] : places[4]]], axis=1
    )
    router_grad = total[:, places[4] : places[4] + experts]

    query_after = tie(query_grad, left, right)
    hidden_grad = (
        nt(query_after, qkv_left) + nt(kv_grad, qkv_right)
    )
    token_norm_grad, attn_gain_grad = norm_back(hidden_grad)
    token_grad = (middle_grad + token_norm_grad)[None]
    gains_sum = grid.everyone(jnp.stack([attn_gain_grad, moe_gain_grad]).reshape(-1, 128))
    gains_sum = gains_sum.reshape(2, grid.count, -1)
    gains_grad = lax.dynamic_index_in_dim(gains_sum, grid.me, 1, keepdims=False).T

    returned = jnp.concatenate(exchange(tie(produced, merged)), axis=0)
    picked = [tn(put[k], returned) for k in range(2)]
    result = middle + combine[:, :1] * picked[0] + combine[:, 1:] * picked[1]
    block_out = result.astype(BF)[None]

    gradients = (qkv_grad, proj_grad, router_grad, gains_grad, gate_up_grad, down_grad)
    firsts = (qkv_first, proj_first, router_first, gains_first, gate_up_first, down_first)
    seconds = (qkv_second, proj_second, router_second, gains_second, gate_up_second, down_second)
    states = [
        adam_ratio(
            owned[number], gradients[number], firsts[number], seconds[number], step_counts[number]
        )
        for number in range(6)
    ]
    weight_sq = jnp.stack([jnp.sum(jnp.square(tensor.astype(F32))) for tensor in owned])
    ratio_sq = jnp.stack([jnp.sum(entry[2] * entry[2]) for entry in states])
    sums_all = grid.everyone(jnp.stack([weight_sq, ratio_sq]))
    weight_tot, ratio_tot = sums_all[0], sums_all[1]
    trust_ratio = jnp.sqrt(weight_tot) * lax.rsqrt(ratio_tot + ratio_epsilon)
    new_weights = [
        owned[number].astype(F32) - learn_rate * trust_ratio[number] * states[number][2]
        for number in range(6)
    ]
    matrix_norms = 0.5 * jnp.log(jnp.stack([weight_tot, ratio_tot + ratio_epsilon]))
    return (
        block_out,
        token_grad,
        *gradients,
        *[entry[0] for entry in states],
        *[entry[1] for entry in states],
        *new_weights,
        matrix_norms,
    )


def solution(mesh):
    rows = P(("ctx", "fsdp"), None)
    tokens = P("fsdp", "ctx", None)
    weights = [rows] * 4 + [tokens] * 2
    return jax.shard_map(
        functools.partial(per_device, mesh.shape["ctx"], mesh.shape["fsdp"]),
        mesh=mesh,
        in_specs=(tokens, P("fsdp", None), tokens, tokens, P())
        + tuple(spec for spec in weights for _ in range(3)),
        out_specs=(tokens, tokens) + tuple(weights) * 4 + (P(),),
        check_vma=False,
    )
```

```python
import functools

import jax
import jax.numpy as jnp
from jax import lax
from jax.experimental import pallas as pl
from jax.experimental.pallas import tpu as pltpu
from jax.sharding import PartitionSpec as P

KEY_HEADS = 8
HEAD_WIDTH = 64
FF = 1024
QUERY_PER_KEY = 3
QUERY_CHANNELS = 1536
KEY_CHANNELS = 512

norm_epsilon = 1e-05
beta_first = 0.9
beta_second = 0.99
adam_epsilon = 1e-08
weight_decay = 0.01
learn_rate = 0.5
ratio_epsilon = 1e-06
score_masked = -1e30
highest_mode = lax.Precision.HIGHEST


BF = jnp.bfloat16
F32 = jnp.float32
AXES = ("ctx", "fsdp")


def rms_norm(values, gain_vec):
    scaling = lax.rsqrt(jnp.mean(values * values, axis=-1, keepdims=True) + norm_epsilon)
    return values * scaling * gain_vec


def routing(logits, chosen):
    probabilities = jax.nn.softmax(logits, axis=-1)
    picked = jnp.sum(jnp.where(chosen, probabilities[:, None, :], 0.0), axis=2)
    return picked / jnp.sum(picked, axis=1, keepdims=True)


def adam_ratio(weight, gradient, first_old, second_old, step_count):
    tensor = weight.astype(F32)
    bias_one = 1.0 - jnp.power(beta_first, step_count)
    bias_two = 1.0 - jnp.power(beta_second, step_count)
    first_new = beta_first * first_old + (1.0 - beta_first) * gradient
    second_new = beta_second * second_old + (1.0 - beta_second) * gradient * gradient
    step_ratio = (
        first_new / bias_one / (jnp.sqrt(second_new / bias_two) + adam_epsilon)
        + weight_decay * tensor
    )
    return (first_new, second_new, step_ratio)


def nt(left, right):
    return lax.dot_general(left, right, (((1,), (1,)), ((), ())), preferred_element_type=F32)


def tn(left, right):
    return lax.dot_general(left, right, (((0,), (0,)), ((), ())), preferred_element_type=F32)


def nn(left, right):
    return jnp.dot(left, right, preferred_element_type=F32)


def tie(value, *others):
    return lax.optimization_barrier((value, *others))[0]


def three_parts(value):
    high = lax.reduce_precision(value, 8, 7)
    rest = value - high
    middle = lax.reduce_precision(rest, 8, 7)
    parts = jnp.concatenate([high, middle, rest - middle], axis=1).astype(BF)
    return jnp.pad(parts, ((0, 0), (0, 125)))


def three(ref, head, rows):
    base = head * QUERY_PER_KEY * HEAD_WIDTH
    return jnp.concatenate(
        [
            ref[:, base + g * HEAD_WIDTH : base + (g + 1) * HEAD_WIDTH]
            for g in range(QUERY_PER_KEY)
        ],
        axis=0,
    )


def put_three(ref, head, rows, turned):
    base = head * QUERY_PER_KEY * HEAD_WIDTH
    for g in range(QUERY_PER_KEY):
        part = turned[:, g * rows : (g + 1) * rows]
        ref[:, base + g * HEAD_WIDTH : base + (g + 1) * HEAD_WIDTH] = part.T.astype(ref.dtype)


def fill_bias(low_ref, bias, rows, window):
    @pl.when(pl.program_id(0) == 0)
    def _():
        def step(block, _):
            start = pl.multiple_of(block * rows, rows)
            key_pos = start + lax.broadcasted_iota(jnp.int32, (rows, rows), 0)
            top = lax.broadcasted_iota(jnp.int32, (rows, rows), 1) + (window - rows)
            allowed = (key_pos >= low_ref[...]) & (key_pos <= top)
            bias[pl.ds(start, rows), :] = jnp.where(allowed, 0.0, score_masked)
            return 0

        lax.fori_loop(0, window // rows, step, 0)


def attend_kernel(first_ref, low_ref, q_ref, k_ref, v_ref, o_ref, turned_ref, lse_ref, bias):
    rows, window = q_ref.shape[0], k_ref.shape[0]
    wide = QUERY_PER_KEY * rows
    fill_bias(low_ref, bias, rows, window)
    first = first_ref[0]
    for head in range(2):
        queries = three(q_ref, head, rows) * jnp.asarray(0.125, BF)
        lanes = slice(head * HEAD_WIDTH, (head + 1) * HEAD_WIDTH)

        def step(block, state):
            top, total, out = state
            span = pl.ds(pl.multiple_of(block * rows, rows), rows)
            shift = bias[span, :]
            scores = nt(k_ref[span, lanes], queries) + jnp.concatenate([shift] * QUERY_PER_KEY, 1)
            top_new = jnp.maximum(top, jnp.max(scores, axis=0, keepdims=True))
            weights = jnp.exp(scores - top_new)
            shrink = jnp.exp(top - top_new)
            total = total * shrink + jnp.sum(weights, axis=0, keepdims=True)
            out = out * shrink + tn(v_ref[span, lanes], weights.astype(BF))
            return (top_new, total, out)

        top, total, out = lax.fori_loop(
            first,
            window // rows,
            step,
            (
                jnp.full((1, wide), score_masked, F32),
                jnp.zeros((1, wide), F32),
                jnp.zeros((HEAD_WIDTH, wide), F32),
            ),
        )
        out = out / total
        turned_ref[head] = out
        lse_ref[head] = top + jnp.log(total)
        put_three(o_ref, head, rows, out)


def attend_grad_kernel(
    first_ref, low_ref, q_ref, k_ref, v_ref, do_ref, turned_ref, lse_ref, dq_ref, dk_ref, dv_ref, bias
):
    rows, window = q_ref.shape[0], k_ref.shape[0]
    wide = QUERY_PER_KEY * rows
    fill_bias(low_ref, bias, rows, window)
    first = first_ref[0]
    dk_ref[...] = jnp.zeros_like(dk_ref)
    dv_ref[...] = jnp.zeros_like(dv_ref)
    for head in range(2):
        queries = three(q_ref, head, rows) * jnp.asarray(0.125, BF)
        grads = three(do_ref, head, rows)
        delta = jnp.sum(grads.astype(F32).T * turned_ref[head], axis=0, keepdims=True)
        norm = lse_ref[head]
        lanes = slice(head * HEAD_WIDTH, (head + 1) * HEAD_WIDTH)

        def step(block, total):
            span = pl.ds(pl.multiple_of(block * rows, rows), rows)
            shift = bias[span, :]
            keys = k_ref[span, lanes]
            scores = nt(keys, queries) + jnp.concatenate([shift] * QUERY_PER_KEY, 1)
            weights = jnp.exp(scores - norm)
            prob_grad = nt(v_ref[span, lanes], grads)
            score_grad = (weights * (prob_grad - delta)).astype(BF)
            dv_ref[span, lanes] = nn(weights.astype(BF), grads).astype(BF)
            dk_ref[span, lanes] = nn(score_grad, queries).astype(BF)
            return total + tn(keys, score_grad)

        total = lax.fori_loop(first, window // rows, step, jnp.zeros((HEAD_WIDTH, wide), F32))
        put_three(dq_ref, head, rows, total * 0.125)


def attention_specs(rows, window):
    pair = 2 * QUERY_PER_KEY * HEAD_WIDTH
    pairs = KEY_HEADS // 2
    q_spec = pl.BlockSpec((rows, pair), lambda p: (0, p))
    k_spec = pl.BlockSpec((window, 2 * HEAD_WIDTH), lambda p: (0, p))
    v_spec = pl.BlockSpec((window, 2 * HEAD_WIDTH), lambda p: (0, p + pairs))
    turned = pl.BlockSpec((2, HEAD_WIDTH, QUERY_PER_KEY * rows), lambda p: (p, 0, 0))
    lse = pl.BlockSpec((2, 1, QUERY_PER_KEY * rows), lambda p: (p, 0, 0))
    first = pl.BlockSpec(memory_space=pltpu.SMEM)
    low = pl.BlockSpec((1, rows), lambda p: (0, 0))
    return pairs, q_spec, k_spec, v_spec, turned, lse, first, low


def attend(first, low, queries, keys_values):
    rows, window = queries.shape[0], keys_values.shape[0]
    pairs, q_spec, k_spec, v_spec, turned, lse, first_spec, low_spec = attention_specs(rows, window)
    wide = QUERY_PER_KEY * rows
    work = KEY_HEADS * wide * window
    return pl.pallas_call(
        attend_kernel,
        grid=(pairs,),
        in_specs=[first_spec, low_spec, q_spec, k_spec, v_spec],
        out_specs=[q_spec, turned, lse],
        out_shape=[
            jax.ShapeDtypeStruct((rows, QUERY_CHANNELS), BF),
            jax.ShapeDtypeStruct((KEY_HEADS, HEAD_WIDTH, wide), F32),
            jax.ShapeDtypeStruct((KEY_HEADS, 1, wide), F32),
        ],
        scratch_shapes=[pltpu.VMEM((window, rows), F32)],
        compiler_params=pltpu.CompilerParams(vmem_limit_bytes=40 << 20),
        cost_estimate=pl.CostEstimate(
            flops=4 * work * HEAD_WIDTH, transcendentals=work, bytes_accessed=8 << 20
        ),
        name="attend",
    )(first, low, queries, keys_values, keys_values)


def attend_grad(first, low, queries, keys_values, out_grad, turned_out, lse_rows):
    rows, window = queries.shape[0], keys_values.shape[0]
    pairs, q_spec, k_spec, v_spec, turned, lse, first_spec, low_spec = attention_specs(rows, window)
    wide = QUERY_PER_KEY * rows
    work = KEY_HEADS * wide * window
    return pl.pallas_call(
        attend_grad_kernel,
        grid=(pairs,),
        in_specs=[first_spec, low_spec, q_spec, k_spec, v_spec, q_spec, turned, lse],
        out_specs=[q_spec, k_spec, k_spec],
        out_shape=[
            jax.ShapeDtypeStruct((rows, QUERY_CHANNELS), BF),
            jax.ShapeDtypeStruct((window, KEY_CHANNELS), BF),
            jax.ShapeDtypeStruct((window, KEY_CHANNELS), BF),
        ],
        scratch_shapes=[pltpu.VMEM((window, rows), F32)],
        compiler_params=pltpu.CompilerParams(vmem_limit_bytes=40 << 20),
        cost_estimate=pl.CostEstimate(
            flops=10 * work * HEAD_WIDTH, transcendentals=work, bytes_accessed=12 << 20
        ),
        name="attend_grad",
    )(first, low, queries, keys_values, keys_values, out_grad, turned_out, lse_rows)


class Grid:
    def __init__(self, ctx, fsdp):
        self.ctx, self.fsdp = ctx, fsdp
        self.count = ctx * fsdp
        self.his = ctx // 2
        self.me = lax.axis_index("ctx") * fsdp + lax.axis_index("fsdp")
        self.lo = lax.rem(lax.axis_index("ctx"), 2)
        self.hi = lax.div(lax.axis_index("ctx"), 2)
        self.lo_mask = fsdp
        self.x_masks = []
        mask = fsdp // 2
        while mask > 1:
            self.x_masks.append(mask)
            mask //= 2

    def swap(self, value, mask):
        return lax.ppermute(value, AXES, [(i, i ^ mask) for i in range(self.count)])

    def shift_hi(self, value, by):
        step = by * 2 * self.fsdp
        pairs = [(i, i + step) for i in range(self.count) if 0 <= i + step < self.count]
        return lax.ppermute(value, AXES, pairs)

    def bit(self, mask):
        return lax.rem(lax.div(self.me, mask), 2)

    def ordered(self, own, got, mask):
        second = self.bit(mask) == 1
        return (jnp.where(second, got, own), jnp.where(second, own, got))

    def gather_hi(self, value):
        return [self.swap(value, m * 2 * self.fsdp) for m in range(1, self.his)]

    def order_hi(self, own, got):
        parts = [own] + got
        span = 1
        while span < self.his:
            odd = lax.rem(lax.div(self.hi, span), 2) == 1
            parts = [jnp.where(odd, parts[j ^ span], parts[j]) for j in range(self.his)]
            span *= 2
        return jnp.stack(parts, axis=0)

    def join(self, value, mask, axis, last=None):
        got = self.swap(value, mask)
        if last is not None:
            got = tie(got, last)
        return jnp.stack(self.ordered(value, got, mask), axis=axis)

    def gather_one(self, held, split, last=None):
        left, right = held[:, :, :split], held[:, :, split:]
        left = self.join(left, self.lo_mask, 1, last)
        for place, mask in enumerate(self.x_masks):
            right = self.join(right, mask, place + 1, last)
        return left, right

    def gather_two(self, left, right, last=None):
        for place, mask in enumerate(self.x_masks):
            left = self.join(left, mask, place + 2, last)
        return left, self.join(right, self.lo_mask, 1, last)

    def gather_core(self, value):
        value = jnp.stack(self.ordered(value, self.swap(value, 1), 1), axis=value.ndim - 2)
        return value.reshape(-1, value.shape[-1])

    def halve(self, value, axis, mask):
        mine = self.bit(mask)
        keep = lax.dynamic_index_in_dim(value, mine, axis, keepdims=False)
        send = lax.dynamic_index_in_dim(value, 1 - mine, axis, keepdims=False)
        got = self.swap(send.astype(BF), mask)
        return keep.astype(F32) + got.astype(F32)

    def scatter_core(self, value):
        bits = len(self.x_masks)
        rows = value.shape[0] // self.count
        value = value.reshape((self.his, 2) + (2,) * bits + (2, rows, value.shape[1]))
        return self.halve(value, 2 + bits, 1)

    def scatter_lo(self, value):
        return self.halve(value, 1, self.lo_mask)

    def scatter_x(self, value, after_lo):
        for mask in self.x_masks:
            value = self.halve(value, 1 if after_lo else 2, mask)
        return value

    def scatter_hi(self, value):
        total = lax.dynamic_index_in_dim(value, self.hi, 0, keepdims=False).astype(F32)
        for m in range(1, self.his):
            other = jnp.bitwise_xor(self.hi, m)
            send = lax.dynamic_index_in_dim(value, other, 0, keepdims=False).astype(BF)
            total = total + self.swap(send, m * 2 * self.fsdp).astype(F32)
        return total

    def everyone(self, value):
        mask = 1
        while mask < self.count:
            value = value + self.swap(value, mask)
            mask *= 2
        return value


def per_device(
    ctx,
    fsdp,
    tokens,
    segment_ids,
    routes,
    upstream,
    step,
    qkv_weight,
    qkv_first,
    qkv_second,
    proj_weight,
    proj_first,
    proj_second,
    router_weight,
    router_first,
    router_second,
    norm_gains,
    gains_first,
    gains_second,
    gate_up,
    gate_up_first,
    gate_up_second,
    down_weight,
    down_first,
    down_second,
):
    grid = Grid(ctx, fsdp)
    rows = tokens.shape[1]
    width = tokens.shape[2]
    seq_len = segment_ids.shape[1]
    experts = router_weight.shape[1]
    capacity = 3 * rows // experts
    hops = (seq_len // 2) // (2 * rows)
    window = (2 * hops + 1) * rows
    groups = [[2 * h + l for h in range(grid.his)] for l in range(2)]
    owned = (qkv_weight, proj_weight, router_weight, norm_gains, gate_up, down_weight)
    step_counts = step.astype(F32)
    lo = grid.lo

    def mine(shards):
        return lax.dynamic_index_in_dim(shards, lo, 0, keepdims=False)

    def others(shards):
        return lax.dynamic_index_in_dim(shards, 1 - lo, 0, keepdims=False)

    def cross(value):
        return grid.swap(value, grid.lo_mask)

    def both_rows(keep, got):
        return jnp.concatenate(grid.ordered(keep, got, grid.lo_mask), axis=0)

    def gather_experts(pair):
        return lax.all_gather(pair, "ctx", axis=0, tiled=True, axis_index_groups=groups)

    small = jnp.concatenate(
        [
            router_weight,
            norm_gains,
            jnp.zeros((router_weight.shape[0], 128 - experts - 2), BF),
        ],
        axis=1,
    )
    split = QUERY_CHANNELS
    half = QUERY_CHANNELS // 2
    qkv_own = jnp.concatenate([qkv_weight, small], axis=1)
    qkv_got = grid.gather_hi(qkv_own)
    own = tokens[0]
    chain = [own, grid.shift_hi(tie(own, qkv_got[0], qkv_got[-1]), 1)]
    gate_up_got = cross(others(gate_up))

    qkv_left, qkv_right = grid.gather_one(grid.order_hi(qkv_own, qkv_got), split)
    for _ in range(1, hops):
        chain.append(grid.shift_hi(tie(chain[-1], qkv_left, qkv_right), 1))
    qkv_left, qkv_right = grid.gather_two(qkv_left, qkv_right)
    across = [cross(jnp.where(lo == 0, own, chain[1]))]
    for k in range(2, hops + 1):
        across.append(cross(tie(jnp.where(lo == 0, chain[k - 1], chain[k]), qkv_left, qkv_right)))
    proj_got = grid.gather_hi(tie(proj_weight, qkv_got[0], qkv_got[-1]))

    gate_up_pair = both_rows(mine(gate_up), gate_up_got)
    full_gate_up = gather_experts(tie(gate_up_pair, chain[hops], qkv_left, qkv_right, *proj_got))

    proj_held = tie(grid.order_hi(proj_weight, proj_got), qkv_left, qkv_right)

    numbers = jnp.arange(experts, dtype=jnp.int32)
    chosen = routes[0][:, :, None] == numbers[None, None, :]
    partners = 2 * fsdp
    flat_routes = routes[0].reshape(-1)
    onehot = (flat_routes[:, None] == numbers[None, :]).astype(jnp.int32)
    earlier = jnp.cumsum(onehot, axis=0) - onehot
    slot_rank = jnp.sum(earlier * onehot, axis=1)
    home = lax.rem(flat_routes, 2) * fsdp + lax.div(flat_routes, 2)
    relative = jnp.bitwise_xor(home, lax.rem(grid.me, partners))
    positions = (relative * capacity + slot_rank).reshape(rows, 2)
    slots = experts * capacity
    slot_ids = jnp.arange(slots, dtype=jnp.int32)
    put = [(slot_ids[:, None] == positions[None, :, k]).astype(BF) for k in range(2)]
    put_both = put[0] + put[1]
    put_wide = jnp.concatenate(put, axis=1)

    def exchange(sent):
        sent = sent.reshape(partners, capacity, sent.shape[1])
        return [sent[0]] + [grid.swap(sent[m], m) for m in range(1, partners)]

    def rows_of(pieces):
        return jnp.concatenate([piece[:, :width] for piece in pieces], axis=0)

    def sides_of(pieces):
        return jnp.concatenate([piece[:, width:] for piece in pieces], axis=0)

    qkv_left = grid.gather_core(qkv_left)
    qkv_right = grid.gather_core(qkv_right)
    full_small = qkv_right[:, 2 * KEY_CHANNELS :]
    qkv_right = qkv_right[:, : 2 * KEY_CHANNELS]
    full_router = full_small[:, :experts]
    full_gains = full_small[:, experts : experts + 2].astype(F32)
    attn_gain, moe_gain = full_gains[:, 0], full_gains[:, 1]

    blocks = [own]
    for k in range(1, hops + 1):
        blocks = [chain[k], across[k - 1]] + blocks
    token_f = own.astype(F32)
    normed, norm_back = jax.vjp(rms_norm, token_f, attn_gain)
    hidden = normed.astype(BF)
    seen = jnp.concatenate(blocks[:-1], axis=0)
    earlier_hidden = rms_norm(seen.astype(F32), attn_gain).astype(BF)
    hidden_window = jnp.concatenate([earlier_hidden, hidden], axis=0)
    queries = nn(hidden, qkv_left).astype(BF)
    keys_values = nn(hidden_window, qkv_right).astype(BF)
    proj_left, proj_right = grid.gather_one(proj_held, half, keys_values)
    proj_left, proj_right = grid.gather_two(proj_left, proj_right)
    down_got = cross(tie(others(down_weight), keys_values))
    full_down = gather_experts(both_rows(mine(down_weight), down_got))
    proj_left = grid.gather_core(proj_left)
    proj_right = grid.gather_core(proj_right)

    segments = segment_ids[0]
    start_own = lax.axis_index("ctx") * rows
    query_seg = lax.dynamic_slice_in_dim(segments, start_own, rows, 0)
    doc_start = jnp.sum((segments[None, :] < query_seg[:, None]).astype(jnp.int32), axis=1)
    low = (doc_start - start_own + (window - rows))[None, :]
    first = lax.div(jnp.maximum(low[0, :1], 0), rows)
    attended, turned_out, lse_rows = attend(first, low, queries, keys_values)

    branch = nt(attended[:, :half], proj_left) + nt(attended[:, half:], proj_right)
    middle = token_f + branch
    second_norm, second_back = jax.vjp(rms_norm, middle, moe_gain)
    second = second_norm.astype(BF)
    logits = nn(second, full_router)
    combine, routing_back = jax.vjp(lambda values: routing(values, chosen), logits)
    wide_rows = jnp.concatenate(
        [
            jnp.concatenate([second, three_parts(combine[:, k : k + 1])], axis=1)
            for k in range(2)
        ],
        axis=0,
    )
    sent_rows = nn(put_wide, wide_rows).astype(BF)
    arrived_pieces = exchange(sent_rows)
    dy_sent = tie(nn(put_both, tie(upstream[0], second)).astype(BF), arrived_pieces[1])
    dy_pieces = exchange(dy_sent)
    arrived = rows_of(arrived_pieces)
    both_parts = nn(arrived, full_gate_up)
    dy_rows = jnp.concatenate([tie(piece, both_parts) for piece in dy_pieces], axis=0)
    shares = jnp.sum(sides_of(arrived_pieces).astype(F32), axis=1, keepdims=True)
    back_arrived = (shares * dy_rows.astype(F32)).astype(BF)
    gates = both_parts[:, :FF]
    ups = both_parts[:, FF:]
    sigmoid_gate = jax.nn.sigmoid(gates)
    silu_gate = gates * sigmoid_gate
    activated = lax.optimization_barrier((silu_gate * ups).astype(BF))

    def reduce_experts(full):
        return lax.psum_scatter(
            full, "ctx", scatter_dimension=0, tiled=True, axis_index_groups=groups
        )

    def own_rows(part):
        part = part.reshape(2, part.shape[0] // 2, part.shape[1])
        both = grid.ordered(mine(part), cross(others(part)), grid.lo_mask)
        return jnp.stack(both, axis=0).astype(F32)

    down_full = tn(activated, back_arrived).astype(BF)
    down_part = reduce_experts(down_full)
    full_down = tie(full_down, down_full)
    act_grad = nt(back_arrived, full_down)
    gate_grad = act_grad * ups * (sigmoid_gate + silu_gate * (1.0 - sigmoid_gate))
    up_grad = act_grad * silu_gate
    both_grad = jnp.concatenate([gate_grad, up_grad], axis=-1).astype(BF)
    produced = nn(activated, full_down).astype(BF)
    share_grads = jnp.sum(produced.astype(F32) * dy_rows.astype(F32), axis=1, keepdims=True)
    row_grads = jnp.concatenate(
        [nt(both_grad, full_gate_up).astype(BF), three_parts(share_grads)], axis=1
    )
    back_pieces = exchange(row_grads)
    gate_up_full = tn(arrived, tie(both_grad, back_pieces[1])).astype(BF)
    gate_up_part = reduce_experts(gate_up_full)
    back_pieces = [tie(piece, gate_up_full) for piece in back_pieces]
    back_returned = rows_of(back_pieces)
    back_sides = sides_of(back_pieces)

    grad_out = upstream[0].astype(F32)
    combine_grad = jnp.stack(
        [jnp.sum(tn(put[k], back_sides), axis=1) for k in range(2)], axis=1
    )
    copy_grads = tn(put_both, back_returned)
    (logit_grad,) = routing_back(combine_grad)
    router_f = full_router.astype(F32)
    second_grad = copy_grads + jnp.dot(
        logit_grad, router_f.T, precision=highest_mode, preferred_element_type=F32
    )
    router_full = jnp.dot(
        logit_grad.T, second.astype(F32), precision=highest_mode, preferred_element_type=F32
    )
    middle_norm_grad, moe_gain_grad = second_back(second_grad)
    middle_grad = grad_out + middle_norm_grad
    middle_low = middle_grad.astype(BF)
    out_grad = jnp.concatenate(
        [nn(middle_low, proj_left).astype(BF), nn(middle_low, proj_right).astype(BF)], axis=1
    )
    proj_cut = KEY_CHANNELS
    proj_one = tn(middle_low, attended[:, :proj_cut]).astype(BF)
    proj_two = tn(middle_low, attended[:, proj_cut:]).astype(BF)
    out_grad = tie(out_grad, proj_one, proj_two)
    proj_one = grid.scatter_core(proj_one)
    proj_two = grid.scatter_core(proj_two)

    query_grad, key_part, value_part = attend_grad(
        first, low, queries, keys_values, out_grad, turned_out, lse_rows
    )
    kv_part = jnp.concatenate([key_part, value_part], axis=1)
    parts = [kv_part[j * rows : (j + 1) * rows] for j in range(2 * hops + 1)]
    crossed = jnp.concatenate([parts[2 * (hops - k) + 1] for k in range(1, hops + 1)], axis=0)
    kept = [parts[2 * hops]] + [parts[2 * (hops - k)] for k in range(1, hops + 1)]
    crossed = cross(crossed)
    got = [None] + [crossed[k * rows : (k + 1) * rows] for k in range(hops)]

    qkv_two = grid.scatter_core(tn(hidden_window, kv_part).astype(BF))
    qkv_one = grid.scatter_core(tn(hidden, query_grad).astype(BF))
    left = jnp.concatenate([qkv_one.astype(BF), proj_one.astype(BF)], axis=-1)
    right = jnp.concatenate([qkv_two.astype(BF), proj_two.astype(BF)], axis=-1)
    left_one = grid.scatter_x(left, False)
    right_one = grid.scatter_lo(right)
    sums = []
    for k in range(hops + 1):
        after = got[k + 1].astype(F32) if k < hops else 0.0
        here = got[k].astype(F32) if k > 0 else 0.0
        sums.append(kept[k].astype(F32) + jnp.where(lo == 1, here, after))
    left_two = grid.scatter_lo(left_one)
    right_two = grid.scatter_x(right_one, True)
    running = tie(sums[hops].astype(BF), left, right)
    for k in range(hops, 0, -1):
        moved = tie(grid.shift_hi(running, -1), left_one, right_one)
        running = (sums[k - 1] + moved.astype(F32)).astype(BF)
    merged = jnp.concatenate([left_two, right_two], axis=-1).astype(BF)
    merged = tie(merged, down_part, gate_up_part)
    kv_grad = tie(running, merged)
    down_grad = own_rows(down_part)
    gate_up_grad = own_rows(gate_up_part)
    total = grid.scatter_hi(merged)
    places = [0, QUERY_CHANNELS, QUERY_CHANNELS + proj_cut]
    places += [places[2] + 2 * KEY_CHANNELS, places[2] + 2 * KEY_CHANNELS + QUERY_CHANNELS - proj_cut]
    qkv_grad = jnp.concatenate([total[:, : places[1]], total[:, places[2] : places[3]]], axis=1)
    proj_grad = jnp.concatenate(
        [total[:, places[1] : places[2]], total[:, places[3] : places[4]]], axis=1
    )

    query_after = tie(query_grad, left, right)
    hidden_grad = (
        nt(query_after, qkv_left) + nt(kv_grad, qkv_right)
    )
    token_norm_grad, attn_gain_grad = norm_back(hidden_grad)
    token_grad = (middle_grad + token_norm_grad)[None]
    weight_sq = jnp.stack([jnp.sum(jnp.square(tensor.astype(F32))) for tensor in owned])
    small_sum = grid.everyone(
        jnp.concatenate(
            [
                jnp.concatenate(
                    [attn_gain_grad[None], moe_gain_grad[None], router_full], axis=0
                ).reshape(-1, 128),
                jnp.pad(weight_sq[None], ((0, 0), (0, 122))),
            ],
            axis=0,
        )
    )
    weight_tot = small_sum[-1, :6]
    small_own = small_sum[:-1].reshape(2 + experts, grid.count, -1)
    small_own = lax.dynamic_index_in_dim(small_own, grid.me, 1, keepdims=False).T
    gains_grad, router_grad = small_own[:, :2], small_own[:, 2:]

    returned = jnp.concatenate(exchange(tie(produced, small_sum)), axis=0)
    picked = [tn(put[k], returned) for k in range(2)]
    result = middle + combine[:, :1] * picked[0] + combine[:, 1:] * picked[1]
    block_out = result.astype(BF)[None]

    gradients = (qkv_grad, proj_grad, router_grad, gains_grad, gate_up_grad, down_grad)
    firsts = (qkv_first, proj_first, router_first, gains_first, gate_up_first, down_first)
    seconds = (qkv_second, proj_second, router_second, gains_second, gate_up_second, down_second)
    states = [
        adam_ratio(
            owned[number], gradients[number], firsts[number], seconds[number], step_counts[number]
        )
        for number in range(6)
    ]
    ratio_sq = jnp.stack([jnp.sum(entry[2] * entry[2]) for entry in states])
    ratio_tot = grid.everyone(ratio_sq[None])[0]
    trust_ratio = jnp.sqrt(weight_tot) * lax.rsqrt(ratio_tot + ratio_epsilon)
    new_weights = [
        owned[number].astype(F32) - learn_rate * trust_ratio[number] * states[number][2]
        for number in range(6)
    ]
    matrix_norms = 0.5 * jnp.log(jnp.stack([weight_tot, ratio_tot + ratio_epsilon]))
    return (
        block_out,
        token_grad,
        *gradients,
        *[entry[0] for entry in states],
        *[entry[1] for entry in states],
        *new_weights,
        matrix_norms,
    )


def solution(mesh):
    rows = P(("ctx", "fsdp"), None)
    tokens = P("fsdp", "ctx", None)
    weights = [rows] * 4 + [tokens] * 2
    return jax.shard_map(
        functools.partial(per_device, mesh.shape["ctx"], mesh.shape["fsdp"]),
        mesh=mesh,
        in_specs=(tokens, P("fsdp", None), tokens, tokens, P())
        + tuple(spec for spec in weights for _ in range(3)),
        out_specs=(tokens, tokens) + tuple(weights) * 4 + (P(),),
        check_vma=False,
    )
```
